32 devices in a mesh: replica: 8 (over z, core), shard: 4 (over y, x).
Axes of the slice: x: 2, y: 2, z: 4, core: 2. Of those that a mesh axis runs over, the one named last changes fastest.
Arguments:
- local_weights: bfloat16 [8, 8192, 512], P('replica', 'shard'), may hold values from -1.3258252 to 1.3258252
- outer_base: bfloat16 [8192, 512], P('shard'), may hold values from -0.0625 to 0.0625
- momentum: bfloat16 [8192, 512], P('shard', 'replica'), may hold values from -0.06591797 to 0.06591797
- error_feedback: bfloat16 [8, 8192, 512], P('replica', 'shard'), may hold values from -0.032958984 to 0.032958984
- q_start: float32 [512, 32], replicated, may hold values from -6 to 6
- tokens: bfloat16 [8, 512, 8192], P('replica', None, 'shard'), may hold values from -6 to 6
Outputs:
- new_base: bfloat16 [8192, 512], P('shard')
- new_momentum: bfloat16 [8192, 512], P('shard', 'replica')
- new_error: bfloat16 [8, 8192, 512], P('replica', 'shard')
- key_rows: bfloat16 [8, 512, 512], P('replica', 'shard')
The draws below stay inside these ranges and needn't reach their ends.
All inputs are finite; a program needn't handle non-finite values.
Results may differ from the reference program's by a relative error of at most 0.0065.
Values may be sent and summed in bfloat16 or wider, within the bound.
A program may use at most 64 MiB of HBM per device.

```python
import jax
import jax.numpy as jnp
from jax import lax

D = 8192
KV = 512
RANK = 32
TOKENS = 512
REPLICAS = 8


def draw_local_weights(key, part):
    key_noise = jax.random.fold_in(key, 11)
    key_rows = jax.random.fold_in(key, 12)
    key_cols = jax.random.fold_in(key, 13)
    noise_val = jax.random.normal(key_noise, (REPLICAS, D, KV), jnp.float32)
    noise_val = jnp.clip(noise_val, -4.0, 4.0)
    rise_rows = 3.0 ** (jnp.arange(D, dtype=jnp.float32) / D)
    row_spread = 10.0 ** jax.random.uniform(key_rows, (D,), jnp.float32)
    col_spread = 10.0 ** jax.random.uniform(key_cols, (KV,), jnp.float32)
    scaled = noise_val * (rise_rows * row_spread)[None, :, None] * col_spread[None, None, :]
    return (scaled * (0.1 * D ** (-0.5))).astype(jnp.bfloat16)


def shard_levels(stream_key, shape, pieces, smallest, largest):
    factor_of, own = 1.0, jax.random.fold_in(stream_key, 6)
    for axis_at, shards_of in pieces:
        heights = jnp.exp(jax.random.uniform(jax.random.fold_in(own, axis_at), (shards_of,), jnp.float32, smallest / len(pieces), largest / len(pieces)))
        factor_of = factor_of * jnp.repeat(heights, shape[axis_at] // shards_of).reshape([-1 if axis == axis_at else 1 for axis in range(len(shape))])
    return factor_of


def gaussian(own_key, dims, width, limit, pieces=(), kind=jnp.bfloat16):
    result = jax.random.normal(own_key, dims, jnp.float32) * width
    if len(pieces) > 0:
        result = shard_levels(own_key, dims, pieces, -0.22, 0.18) * result
    return jnp.clip(result, min=-limit, max=limit).astype(kind)


def setup_inputs(seed: int = 0) -> dict:
    key_list = jax.random.split(jax.random.key(seed), 7)
    return {
        "local_weights": draw_local_weights(jax.random.fold_in(key_list[6], 71), 0),
        "outer_base": gaussian(key_list[1], (D, KV), D ** -0.5, 0.0625, ((0, 4),)),
        "momentum": gaussian(key_list[2], (D, KV), (D ** -0.5), 0.06591797, ((0, 4), (1, 8))),
        "error_feedback": gaussian(key_list[3], (REPLICAS, D, KV), (0.5 * D ** -0.5), 0.032958984, ((0, 8), (1, 4))),
        "q_start": gaussian(key_list[4], (KV, RANK), 1.0, 6.0, (), jnp.float32),
        "tokens": gaussian(key_list[5], (REPLICAS, TOKENS, D), 1.0, 6.0, ((0, 8), (2, 4))),
    }


outer_mu = 0.9
outer_rate = 0.7

def reference(local_weights, outer_base, momentum, error_feedback, q_start, tokens):
    highest = lax.Precision.HIGHEST
    pseudo = outer_base.astype(jnp.float32)[None] - local_weights.astype(jnp.float32) + error_feedback.astype(jnp.float32)
    p_mean = jnp.einsum('rdk,kq->dq', pseudo, q_start, precision=highest) / REPLICAS
    gram = jnp.dot(p_mean.T, p_mean, precision=highest)
    factor_low = jnp.linalg.cholesky(gram)
    basis = jax.scipy.linalg.solve_triangular(factor_low, p_mean.T, lower=True).T
    q_mean = jnp.einsum('rdk,dq->kq', pseudo, basis, precision=highest) / REPLICAS
    update = jnp.dot(basis, q_mean.T, precision=highest)
    new_error = (pseudo - update[None]).astype(jnp.bfloat16)
    moment = outer_mu * momentum.astype(jnp.float32) + update
    new_base = (outer_base.astype(jnp.float32) - outer_rate * (outer_mu * moment + update)).astype(jnp.bfloat16)

    def project(token_block):
        return jnp.dot(token_block.astype(jnp.float32), new_base.astype(jnp.float32), preferred_element_type=jnp.float32).astype(jnp.bfloat16)
    key_rows = lax.map(project, tokens)
    return (new_base, moment.astype(jnp.bfloat16), new_error, key_rows)
```

```python
import functools

import jax
import jax.numpy as jnp
from jax import lax
from jax.experimental import pallas as pl
from jax.experimental.pallas import tpu as pltpu
from jax.sharding import PartitionSpec as P

outer_mu = 0.9
outer_rate = 0.7
MESH = pl.DeviceIdType.MESH
F32 = jnp.float32
BF16 = jnp.bfloat16
NT = (((1,), (1,)), ((), ()))
NN = (((1,), (0,)), ((), ()))
TN = (((0,), (0,)), ((), ()))
HIGHEST = lax.Precision.HIGHEST
HALVES = 2


def dot(a, b, dims):
    return lax.dot_general(a, b, dims, preferred_element_type=F32)


def split2(x):
    high = x.astype(BF16)
    return high, (x - high.astype(F32)).astype(BF16)


def invert(a):
    n = a.shape[0]
    rows = lax.broadcasted_iota(jnp.int32, (n, n), 0)
    cols = lax.broadcasted_iota(jnp.int32, (n, n), 1)
    lane = lax.broadcasted_iota(jnp.int32, (1, n), 1)
    for k in range(n):
        inverse_pivot = 1.0 / a[k : k + 1, k : k + 1]
        col = a[:, k : k + 1]
        row = jnp.where(lane == k, 1.0, a[k : k + 1, :]) * inverse_pivot
        a = jnp.where(rows == k, row, jnp.where(cols == k, 0.0, a) - col * row)
    return a


def sizes(d, kv, rank, S):
    h = d // 2
    nc = 2 if h % 256 == 0 else 1
    groups = min(S, rank // 8)
    return h, nc, h // nc, groups, rank // groups, kv // (S // groups)


def exchange(cfg, lw, base, ef, qt, mom, tok, nb_out, nm_out, ne_out, key_out,
             lw_v, base_v, ef_v, zh, zl, tok_v, slots, mom_rows, v_buf,
             pt, pair_in, half, half_bf, rs_in, pm, gs, g_in,
             tl, t_in, ts, qp_in, z_in, tt, x2, xo2, a_buf, a_bf, a_in, bt, b_in,
             ld_sem, mom_ld, pair_sem, rs_send, rs_recv, ag_send, ag_recv, fw_send,
             g_send, g_recv, t_send, t_recv, qp_sem, z_send, z_recv, ta_send, ta_recv,
             own_send, fz_send, fp_send, m_recv, a_send, a_recv, b_send, b_recv):
    R, S, d, kv, rank = cfg
    L = R // 2
    me = lax.axis_index("replica")
    shard = lax.axis_index("shard")
    core = lax.rem(me, 2)
    pos = me // 2
    partner = me + 1 - 2 * core
    chunks = ld_sem.shape[1]
    rows = d // chunks
    h, nc, w, groups, tile_rows, wl = sizes(d, kv, rank, S)
    first_owner = L // 2 - nc // 2
    c = slots.shape[1]
    per = 128 // c
    blocks = kv // 128
    n = tok_v.shape[0] // S
    early = per == 2
    HV = HALVES
    span = d // HV

    def at_replica(r):
        return {"replica": r}

    def at_shard(s):
        return {"shard": s}

    def block_of(p):
        return 2 * p + core

    def rcopy(src, dst, ss, rs, dev):
        return pltpu.make_async_remote_copy(src_ref=src, dst_ref=dst, send_sem=ss, recv_sem=rs,
                                            device_id=dev, device_id_type=MESH)

    barrier = pltpu.get_barrier_semaphore()
    for k in range(1, R):
        pl.semaphore_signal(barrier, inc=1, device_id=at_replica(lax.rem(me + k, R)), device_id_type=MESH)
    for k in range(1, S):
        pl.semaphore_signal(barrier, inc=1, device_id=at_shard(lax.rem(shard + k, S)), device_id_type=MESH)

    loads = []
    for k in range(chunks):
        trio = []
        for i, (src, dst) in enumerate(((lw, lw_v), (base, base_v), (ef, ef_v))):
            part = pl.ds(k * rows, rows)
            cp = pltpu.make_async_copy(src.at[part], dst.at[part], ld_sem.at[i, k])
            cp.start()
            trio.append(cp)
        loads.append(trio)
    own_in = pltpu.make_async_copy(mom, slots.at[me], mom_ld.at[0])
    own_in.start()
    tok_in = pltpu.make_async_copy(tok, tok_v, mom_ld.at[1])
    tok_in.start()

    def slot(b, hv):
        return slots.at[b, :, pl.ds(hv * span, span)]

    def own_copies(hv, act):
        def go(i, target):
            act(rcopy(slot(me, hv), slot(me, hv), own_send.at[i, hv], m_recv.at[me, hv], at_replica(target)))

        @pl.when(pos + 1 < L)
        def _():
            go(0, block_of(jnp.minimum(pos + 1, L - 1)))

        @pl.when(pos >= 1)
        def _():
            go(1, block_of(jnp.maximum(pos - 1, 0)))

        if L > 2:
            @pl.when((pos == 0) | (pos == L - 1))
            def _():
                go(2, block_of(jnp.where(pos == 0, 2, L - 3)))

        go(3, partner)

    def start(cp):
        cp.start()

    def finish_send(cp):
        cp.wait_send()

    def await_half(b, hv):
        rcopy(slot(b, hv), slot(b, hv), own_send.at[0, hv], m_recv.at[b, hv], at_replica(partner)).wait_recv()

    def passed_on(step, hv, act, wait):
        for side, sign in enumerate((-1, 1)):
            origin = pos + sign * step
            nxt = pos - sign
            end = 0 if side == 0 else L - 1

            @pl.when((origin >= 0) & (origin < L))
            def _():
                b = block_of(jnp.clip(origin, 0, L - 1))
                if wait:
                    await_half(b, hv)
                here = (nxt >= 0) & (nxt < L)
                if step == 1:
                    here = here & (origin != end)

                @pl.when(here)
                def _():
                    act(rcopy(slot(b, hv), slot(b, hv), fz_send.at[side, step - 1, hv], m_recv.at[b, hv],
                              at_replica(block_of(jnp.clip(nxt, 0, L - 1)))))

                act(rcopy(slot(b, hv), slot(b, hv), fp_send.at[side, step - 1, hv], m_recv.at[b, hv],
                          at_replica(partner)))

    def arrived(step, hv):
        if step < L:
            passed_on(step, hv, start, True)

    def token_rows(s):
        return pl.ds(pl.multiple_of(s * n, 128), n)

    def block_cols(bk):
        return pl.ds(pl.multiple_of(bk * 128, 128), 128)

    def a_copy(k, bk):
        target = lax.rem(shard + k, S)
        return rcopy(a_bf.at[token_rows(target), block_cols(bk)], a_in.at[shard, :, block_cols(bk)],
                     a_send.at[k, bk], a_recv.at[shard, bk], at_shard(target))

    def key_block(bk):
        cols = block_cols(bk)
        block = slots[pl.ds(bk * per, per)].reshape(128, d)
        a = a_buf[:, cols] - (outer_rate * outer_mu * outer_mu) * dot(tok_v[...], block, NT)
        a_buf[:, cols] = a
        a_bf[:, cols] = a.astype(BF16)
        for k in range(1, S):
            a_copy(k, bk).start()

    def turn_block(bk):
        mom_rows[:, block_cols(bk)] = slots[pl.ds(bk * per, per)].reshape(128, d).T

    def chip_block(p):
        for hv in range(HV):
            await_half(2 * p + 1 - core, hv)

    def blocks_at(step, f):
        def side(i, carry):
            origin = pos + (2 * i - 1) * step

            @pl.when((origin >= 0) & (origin < L))
            def _():
                f(jnp.clip(origin, 0, L - 1))

            return carry

        lax.fori_loop(0, 2, side, 0)

    def take_block(p):
        chip_block(p)
        if early:
            key_block(p)

    def take_and_turn(p):
        take_block(p)
        if early:
            turn_block(p)

    qh, ql = split2(qt[...])
    q2 = jnp.concatenate([qh, ql], axis=0)
    for k in range(chunks):
        for cp in loads[k]:
            cp.wait()
        part = pl.ds(k * rows, rows)
        z = base_v[part, :].astype(F32) - lw_v[part, :].astype(F32) + ef_v[part, :].astype(F32)
        high, low = split2(z)
        zh[part, :] = high
        zl[part, :] = low
        both = dot(q2, high, NT)
        pt[:, part] = both[:rank] + (both[rank:] + dot(qh, low, NT))

    own_in.wait()
    pl.semaphore_wait(barrier, R - 1 + S - 1)

    theirs = pl.ds(pl.multiple_of((1 - core) * h, 128), h)
    mine = pl.ds(pl.multiple_of(core * h, 128), h)
    pair = rcopy(pt.at[:, theirs], pair_in, pair_sem.at[0], pair_sem.at[1], at_replica(partner))
    pair.start()
    own_copies(0, start)
    pair.wait_recv()
    total = pt[:, mine] + pair_in[...]
    half[...] = total
    half_bf[...] = total.astype(BF16)

    def rs_copies(act):
        for j in range(nc):
            target = first_owner + j

            @pl.when(pos != target)
            def _():
                act(rcopy(half_bf.at[:, pl.ds(j * w, w)], rs_in.at[pos], rs_send.at[j], rs_recv.at[pos],
                          at_replica(block_of(target))))

    rs_copies(start)
    for hv in range(1, HV):
        own_copies(hv, start)

    owner = (pos >= first_owner) & (pos < first_owner + nc)
    own_index = jnp.clip(pos - first_owner, 0, nc - 1)

    def cols_of(cr, j):
        return pl.ds(pl.multiple_of(cr * h + j * w, 128), w)

    def fw_copy(cr, j):
        part = pm.at[:, cols_of(cr, j)]
        return rcopy(part, part, fw_send.at[j], ag_recv.at[cr, j], at_replica(partner))

    def ag_copy(k):
        part = pm.at[:, cols_of(core, own_index)]
        return rcopy(part, part, ag_send.at[k], ag_recv.at[core, own_index],
                     at_replica(block_of(lax.rem(pos + k, L))))

    tok_in.wait()
    a_buf[...] = dot(tok_v[...], base_v[...], NN)

    @pl.when(owner)
    def _():
        total = half[:, pl.ds(pl.multiple_of(own_index * w, 128), w)]
        for k in range(1, L):
            source = lax.rem(pos + k, L)
            rcopy(rs_in.at[source], rs_in.at[source], ag_send.at[k], rs_recv.at[source],
                  at_replica(partner)).wait_recv()
            total += rs_in[source].astype(F32)
        pm[:, cols_of(core, own_index)] = (total * (1.0 / R)).astype(BF16)
        for k in range(1, L):
            ag_copy(k).start()
        for j in range(nc):
            @pl.when(pos == first_owner + j)
            def _():
                fw_copy(core, j).start()

    arrived(1, 0)
    for j in range(nc):
        @pl.when(pos != first_owner + j)
        def _():
            fw_copy(core, j).wait_recv()
            fw_copy(core, j).start()
    chip_block(pos)
    if early:
        turn_block(pos)
    for j in range(nc):
        fw_copy(1 - core, j).wait_recv()

    tl[...] = dot(pm[...], zh[...], NN) + dot(pm[...], zl[...], NN)

    def tile_of(s):
        return (pl.ds(pl.multiple_of(lax.rem(s, groups) * tile_rows, 8), tile_rows),
                pl.ds(pl.multiple_of((s // groups) * wl, 128), wl))

    def t_copy(k):
        target = lax.rem(shard + k, S)
        a, b = tile_of(target)
        return rcopy(tl.at[a, b], t_in.at[shard], t_send.at[k], t_recv.at[shard], at_shard(target))

    for k in range(1, S):
        t_copy(k).start()
    for hv in range(1, HV):
        arrived(1, hv)
    gs[...] = jnp.zeros_like(gs)
    gs[:, 0:rank] = dot(pm[...], pm[...], NT)

    def g_copy(k):
        return rcopy(gs, g_in.at[shard], g_send.at[k], g_recv.at[shard], at_shard(lax.rem(shard + k, S)))

    for k in range(1, S):
        g_copy(k).start()
    my_rows, my_cols = tile_of(shard)
    total = tl[my_rows, my_cols]
    for k in range(1, S):
        source = lax.rem(shard + k, S)
        rcopy(t_in.at[source], t_in.at[source], t_send.at[k], t_recv.at[source], at_replica(partner)).wait_recv()
        total += t_in[source]
    ts[...] = total
    q_pair = rcopy(ts, qp_in, qp_sem.at[0], qp_sem.at[1], at_replica(partner))
    q_pair.start()
    bt[...] = dot(pm[...], tok_v[...], NT)

    def b_copy(k):
        target = lax.rem(shard + k, S)
        return rcopy(bt.at[:, token_rows(target)], b_in.at[shard], b_send.at[k], b_recv.at[shard], at_shard(target))

    for k in range(1, S):
        b_copy(k).start()
    q_pair.wait_recv()
    z_in[pos] = ts[...] + qp_in[...]

    def z_copy(k):
        part = z_in.at[pos]
        return rcopy(part, part, z_send.at[k], z_recv.at[pos], at_replica(block_of(lax.rem(pos + k, L))))

    for k in range(1, L):
        z_copy(k).start()
    arrived(2, 0)
    if early:
        key_block(pos)
    for k in range(1, L):
        source = lax.rem(pos + k, L)
        rcopy(z_in.at[source], z_in.at[source], z_send.at[k], z_recv.at[source], at_replica(partner)).wait_recv()
    total = z_in[0]
    for p in range(1, L):
        total += z_in[p]
    tt[my_rows, my_cols] = total * (1.0 / R)

    def ta_copy(k):
        part = tt.at[my_rows, my_cols]
        return rcopy(part, part, ta_send.at[k], ta_recv.at[shard], at_shard(lax.rem(shard + k, S)))

    for k in range(1, S):
        ta_copy(k).start()
    for hv in range(1, HV):
        arrived(2, hv)
    if L > 1:
        blocks_at(1, take_and_turn)

    gram = gs[:, 0:rank]
    for k in range(1, S):
        source = lax.rem(shard + k, S)
        rcopy(g_in.at[source], g_in.at[source], g_send.at[k], g_recv.at[source], at_replica(partner)).wait_recv()
        gram = gram + g_in[source][:, 0:rank]
    inverse = invert(gram)
    for step in range(2, L - 1):
        if step > 2:
            for hv in range(HV):
                arrived(step, hv)
        blocks_at(step, take_and_turn)

    for k in range(1, S):
        source = lax.rem(shard + k, S)
        a, b = tile_of(source)
        rcopy(tt.at[a, b], tt.at[a, b], ta_send.at[k], ta_recv.at[source], at_replica(partner)).wait_recv()
    x = lax.dot_general(inverse, tt[...], NN, precision=HIGHEST, preferred_element_type=F32)
    high, low = split2(x)
    x2[...] = jnp.concatenate([high, low], axis=0)
    pick = (lax.broadcasted_iota(jnp.int32, (kv, c), 0)
            == me * c + lax.broadcasted_iota(jnp.int32, (kv, c), 1)).astype(BF16)
    xo2[...] = dot(x2[...], pick, NN).astype(BF16)

    tile = min(256, d)

    def update_rows(t, carry):
        part = pl.ds(pl.multiple_of(t * tile, 128), tile)
        p = pm[:, part]
        p2 = jnp.concatenate([p, p], axis=0)
        u = dot(p2, x2[...], TN)
        ne_out[part, :] = ((zh[part, :].astype(F32) + zl[part, :].astype(F32)) - u).astype(BF16)
        v_buf[part, :] = base_v[part, :].astype(F32) - (outer_rate * (outer_mu + 1.0)) * u
        nm_out[:, part] = (outer_mu * slots[me, :, part].astype(F32) + dot(xo2[...], p2, TN)).astype(BF16)
        return carry

    lax.fori_loop(0, d // tile, update_rows, 0)

    if L > 3:
        for hv in range(HV):
            arrived(L - 1, hv)
    if L > 2:
        blocks_at(L - 1, take_and_turn)
    if not early:
        def late(bk, carry):
            key_block(bk)
            turn_block(bk)
            return carry

        lax.fori_loop(0, blocks, late, 0)

    def base_rows(t, carry):
        part = pl.ds(pl.multiple_of(t * tile, 128), tile)
        nb_out[part, :] = (v_buf[part, :] - (outer_rate * outer_mu * outer_mu) * mom_rows[part, :].astype(F32)).astype(BF16)
        return carry

    lax.fori_loop(0, d // tile, base_rows, 0)

    b_total = bt[:, token_rows(shard)]
    for k in range(1, S):
        source = lax.rem(shard + k, S)
        rcopy(b_in.at[source], b_in.at[source], b_send.at[k], b_recv.at[source], at_replica(partner)).wait_recv()
        b_total += b_in[source]
    total = a_buf[token_rows(shard), :] - (outer_rate * (outer_mu + 1.0)) * lax.dot_general(
        b_total, x, TN, precision=HIGHEST, preferred_element_type=F32)
    for k in range(1, S):
        source = lax.rem(shard + k, S)
        for bk in range(blocks):
            part = a_in.at[source, :, block_cols(bk)]
            rcopy(part, part, a_send.at[k, bk], a_recv.at[source, bk], at_replica(partner)).wait_recv()
        total += a_in[source].astype(F32)
    key_out[...] = total.astype(BF16)

    for hv in range(HV):
        own_copies(hv, finish_send)
        for step in range(1, L):
            passed_on(step, hv, finish_send, False)
    for k in range(1, S):
        for bk in range(blocks):
            a_copy(k, bk).wait_send()
        b_copy(k).wait_send()
        g_copy(k).wait_send()
        t_copy(k).wait_send()
        ta_copy(k).wait_send()
    pair.wait_send()
    q_pair.wait_send()
    rs_copies(finish_send)
    for k in range(1, L):
        z_copy(k).wait_send()
    for j in range(nc):
        fw_copy(core, j).wait_send()

    @pl.when(owner)
    def _():
        for k in range(1, L):
            ag_copy(k).wait_send()


def store(nb, nm, ne, key, nb_out, nm_out, ne_out, key_out, sem):
    copies = [pltpu.make_async_copy(s, o, sem.at[i]) for i, (s, o) in
              enumerate(((nb, nb_out), (ne, ne_out), (nm, nm_out), (key, key_out)))]
    for cp in copies:
        cp.start()
    for cp in copies:
        cp.wait()


def on_device(local_weights, outer_base, momentum, error_feedback, q_start, tokens):
    R = lax.axis_size("replica")
    S = lax.axis_size("shard")
    d, kv = outer_base.shape
    rank = q_start.shape[1]
    c = momentum.shape[1]
    L = R // 2
    lw, ef, tok = local_weights[0], error_feedback[0], tokens[0]
    nt = tok.shape[0]
    n = nt // S
    blocks = kv // 128
    chunks = min(4, d // 128)
    h, nc, w, groups, tile_rows, wl = sizes(d, kv, rank, S)
    HV = HALVES
    V = pltpu.VMEM
    dma = pltpu.SemaphoreType.DMA
    hbm = pl.BlockSpec(memory_space=pltpu.HBM)
    anywhere = pl.BlockSpec(memory_space=pl.ANY)
    vm = pl.BlockSpec(memory_space=pltpu.VMEM)
    shapes = ((d, kv), (c, d), (d, kv), (n, kv))
    held = pl.pallas_call(
        functools.partial(exchange, (R, S, d, kv, rank)),
        out_shape=tuple(pltpu.VMEM(s, BF16) for s in shapes),
        in_specs=[hbm, hbm, hbm, vm, hbm, hbm],
        out_specs=(vm,) * 4,
        scratch_shapes=[
            V((d, kv), BF16), V((d, kv), BF16), V((d, kv), BF16), V((d, kv), BF16), V((d, kv), BF16),
            V((nt, d), BF16), V((R, c, d), BF16), V((d, kv), BF16), V((d, kv), F32),
            V((rank, d), F32), V((rank, h), F32), V((rank, h), F32), V((rank, h), BF16), V((L, rank, w), BF16),
            V((rank, d), BF16), V((rank, 128), F32), V((S, rank, 128), F32),
            V((rank, kv), F32), V((S, tile_rows, wl), F32), V((tile_rows, wl), F32), V((tile_rows, wl), F32),
            V((L, tile_rows, wl), F32), V((rank, kv), F32), V((2 * rank, kv), BF16), V((2 * rank, c), BF16),
            V((nt, kv), F32), V((nt, kv), BF16), V((S, n, kv), BF16), V((rank, nt), F32), V((S, rank, n), F32),
            dma((3, chunks)), dma((2,)), dma((2,)), dma((nc,)), dma((L,)), dma((L,)), dma((2, nc)), dma((nc,)),
            dma((S,)), dma((S,)), dma((S,)), dma((S,)), dma((2,)), dma((L,)), dma((L,)), dma((S,)), dma((S,)),
            dma((4, HV)), dma((2, L, HV)), dma((2, L, HV)), dma((R, HV)),
            dma((S, blocks)), dma((S, blocks)), dma((S,)), dma((S,)),
        ],
        compiler_params=pltpu.CompilerParams(collective_id=0, has_side_effects=True, vmem_limit_bytes=52 << 20),
        name="exchange",
    )(lw, outer_base, ef, q_start.T, momentum.T, tok)
    nb, nm, ne, keys = pl.pallas_call(
        store,
        out_shape=tuple(jax.ShapeDtypeStruct(s, BF16) for s in shapes),
        in_specs=[vm] * 4,
        out_specs=(anywhere,) * 4,
        scratch_shapes=[dma((4,))],
        compiler_params=pltpu.CompilerParams(vmem_limit_bytes=4 << 20),
        name="store",
    )(*held)
    return nb, nm.T, ne[None], keys[None]


def solution(mesh):
    in_specs = (
        P("replica", "shard", None),
        P("shard", None),
        P("shard", "replica"),
        P("replica", "shard", None),
        P(),
        P("replica", None, "shard"),
    )
    out_specs = (
        P("shard", None),
        P("shard", "replica"),
        P("replica", "shard", None),
        P("replica", "shard", None),
    )
    return jax.shard_map(
        on_device, mesh=mesh, in_specs=in_specs, out_specs=out_specs, check_vma=False
    )
```

```python
import functools

import jax
import jax.numpy as jnp
from jax import lax
from jax.experimental import pallas as pl
from jax.experimental.pallas import tpu as pltpu
from jax.sharding import PartitionSpec as P

outer_mu = 0.9
outer_rate = 0.7
MESH = pl.DeviceIdType.MESH
F32 = jnp.float32
BF16 = jnp.bfloat16
NT = (((1,), (1,)), ((), ()))
NN = (((1,), (0,)), ((), ()))
TN = (((0,), (0,)), ((), ()))
HIGHEST = lax.Precision.HIGHEST
HALVES = 4


def dot(a, b, dims):
    return lax.dot_general(a, b, dims, preferred_element_type=F32)


def split2(x):
    high = x.astype(BF16)
    return high, (x - high.astype(F32)).astype(BF16)


def invert(a):
    n = a.shape[0]
    rows = lax.broadcasted_iota(jnp.int32, (n, n), 0)
    cols = lax.broadcasted_iota(jnp.int32, (n, n), 1)
    lane = lax.broadcasted_iota(jnp.int32, (1, n), 1)
    for k in range(n):
        inverse_pivot = 1.0 / a[k : k + 1, k : k + 1]
        col = a[:, k : k + 1]
        row = jnp.where(lane == k, 1.0, a[k : k + 1, :]) * inverse_pivot
        a = jnp.where(rows == k, row, jnp.where(cols == k, 0.0, a) - col * row)
    return a


def sizes(d, kv, rank, S):
    h = d // 2
    nc = 2 if h % 256 == 0 else 1
    groups = rank // 8
    tiles = min(2 * S, groups * (kv // 128))
    return h, nc, h // nc, groups, tiles, kv // (tiles // groups)


def exchange(cfg, lw, base, ef, qt, mom, tok, nb_out, nm_out, ne_out, key_out,
             lw_v, base_v, ef_v, zh, zh_in, zs, zf, tok_v, slots, v_buf,
             pt, pair_in, half, half_bf, rs_in, pm, gs, g_in,
             tl, t_in, z_in, tt, x2, xo2, a_buf, a_bf, a_in, bt, b_in,
             ld_sem, mom_ld, pair_sem, zx_sem, rs_send, rs_recv, ag_send, ag_recv, fw_send,
             g_send, g_recv, t_send, t_recv, z_send, z_recv, ta_send, ta_recv,
             own_send, fz_send, fp_send, m_recv, a_send, a_recv, b_send, b_recv):
    R, S, d, kv, rank = cfg
    L = R // 2
    me = lax.axis_index("replica")
    shard = lax.axis_index("shard")
    core = lax.rem(me, 2)
    pos = me // 2
    partner = me + 1 - 2 * core
    chunks = ld_sem.shape[1]
    rows = d // chunks
    h, nc, w, groups, tiles, wl = sizes(d, kv, rank, S)
    first_owner = L // 2 - nc // 2
    c = slots.shape[1]
    per = 128 // c
    blocks = kv // 128
    n = tok_v.shape[0] // S
    early = per == 2
    HV = HALVES
    span = d // HV
    plane = 2 * S
    spot = 2 * shard + core

    def at_replica(r):
        return {"replica": r}

    def at_shard(s):
        return {"shard": s}

    def at_spot(i):
        return {"replica": 2 * pos + lax.rem(i, 2), "shard": i // 2}

    def block_of(p):
        return 2 * p + core

    def rcopy(src, dst, ss, rs, dev):
        return pltpu.make_async_remote_copy(src_ref=src, dst_ref=dst, send_sem=ss, recv_sem=rs,
                                            device_id=dev, device_id_type=MESH)

    barrier = pltpu.get_barrier_semaphore()
    for k in range(1, R):
        pl.semaphore_signal(barrier, inc=1, device_id=at_replica(lax.rem(me + k, R)), device_id_type=MESH)
    for k in range(1, S):
        for r in (me, partner):
            pl.semaphore_signal(barrier, inc=1, device_id={"replica": r, "shard": lax.rem(shard + k, S)},
                                device_id_type=MESH)

    loads = []
    for k in range(chunks):
        trio = []
        for i, (src, dst) in enumerate(((lw, lw_v), (base, base_v), (ef, ef_v))):
            part = pl.ds(k * rows, rows)
            cp = pltpu.make_async_copy(src.at[part], dst.at[part], ld_sem.at[i, k])
            cp.start()
            trio.append(cp)
        loads.append(trio)
    own_in = pltpu.make_async_copy(mom, slots.at[me], mom_ld.at[0])
    own_in.start()
    tok_in = pltpu.make_async_copy(tok, tok_v, mom_ld.at[1])
    tok_in.start()

    def slot(b, hv):
        return slots.at[b, :, pl.ds(hv * span, span)]

    def own_copies(hv, act):
        def go(i, target):
            act(rcopy(slot(me, hv), slot(me, hv), own_send.at[i, hv], m_recv.at[me, hv], at_replica(target)))

        @pl.when(pos + 1 < L)
        def _():
            go(0, block_of(jnp.minimum(pos + 1, L - 1)))

        @pl.when(pos >= 1)
        def _():
            go(1, block_of(jnp.maximum(pos - 1, 0)))

        if L > 2:
            @pl.when((pos == 0) | (pos == L - 1))
            def _():
                go(2, block_of(jnp.where(pos == 0, 2, L - 3)))

    def own_to_partner(hv):
        return rcopy(slot(me, hv), slot(me, hv), own_send.at[3, hv], m_recv.at[me, hv], at_replica(partner))

    def start(cp):
        cp.start()

    def finish_send(cp):
        cp.wait_send()

    def await_half(b, hv):
        rcopy(slot(b, hv), slot(b, hv), own_send.at[0, hv], m_recv.at[b, hv], at_replica(partner)).wait_recv()

    def passed_on(step, hv, act, wait):
        for side, sign in enumerate((-1, 1)):
            origin = pos + sign * step
            nxt = pos - sign
            end = 0 if side == 0 else L - 1

            @pl.when((origin >= 0) & (origin < L))
            def _():
                b = block_of(jnp.clip(origin, 0, L - 1))
                if wait:
                    await_half(b, hv)
                here = (nxt >= 0) & (nxt < L)
                if step == 1:
                    here = here & (origin != end)

                @pl.when(here)
                def _():
                    act(rcopy(slot(b, hv), slot(b, hv), fz_send.at[side, step - 1, hv], m_recv.at[b, hv],
                              at_replica(block_of(jnp.clip(nxt, 0, L - 1)))))

                act(rcopy(slot(b, hv), slot(b, hv), fp_send.at[side, step - 1, hv], m_recv.at[b, hv],
                          at_replica(partner)))

    def arrived(step, *parts):
        if step < L:
            for hv in parts:
                passed_on(step, hv, start, True)

    def token_rows(s):
        return pl.ds(pl.multiple_of(s * n, 128), n)

    def block_cols(bk):
        return pl.ds(pl.multiple_of(bk * 128, 128), 128)

    def a_copy(k, bk):
        target = lax.rem(shard + k, S)
        return rcopy(a_bf.at[token_rows(target), block_cols(bk)], a_in.at[shard, :, block_cols(bk)],
                     a_send.at[k, bk], a_recv.at[shard, bk], at_shard(target))

    def key_block(bk):
        cols = block_cols(bk)
        block = slots[pl.ds(bk * per, per)].reshape(128, d)
        a = a_buf[:, cols] - (outer_rate * outer_mu * outer_mu) * dot(tok_v[...], block, NT)
        a_buf[:, cols] = a
        a_bf[:, cols] = a.astype(BF16)
        for k in range(1, S):
            a_copy(k, bk).start()

    def turn_block(bk):
        cols = block_cols(bk)
        turned = slots[pl.ds(bk * per, per)].reshape(128, d).T
        v_buf[:, cols] = base_v[:, cols].astype(F32) - (outer_rate * outer_mu * outer_mu) * turned.astype(F32)

    def chip_block(p):
        for hv in range(HV):
            await_half(2 * p + 1 - core, hv)

    def blocks_at(step, *fs):
        if not 0 < step < L:
            return

        def side(i, carry):
            origin = pos + (2 * i - 1) * step

            @pl.when((origin >= 0) & (origin < L))
            def _():
                for f in fs:
                    f(jnp.clip(origin, 0, L - 1))

            return carry

        lax.fori_loop(0, 2, side, 0)

    keys_of = key_block if early else lambda p: None
    turn_of = turn_block if early else lambda p: None
    quarters = tuple(range(HV))
    first, second = quarters[: HV // 2], quarters[HV // 2 :]

    qh, ql = split2(qt[...])
    q2 = jnp.concatenate([qh, ql], axis=0)
    for k in range(chunks):
        for cp in loads[k]:
            cp.wait()
        part = pl.ds(k * rows, rows)
        z = base_v[part, :].astype(F32) - lw_v[part, :].astype(F32) + ef_v[part, :].astype(F32)
        zf[part, :] = z
        high, low = split2(z)
        zh[part, :] = high
        both = dot(q2, high, NT)
        pt[:, part] = both[:rank] + (both[rank:] + dot(qh, low, NT))

    own_in.wait()
    pl.semaphore_wait(barrier, R - 1 + 2 * (S - 1))

    theirs = pl.ds(pl.multiple_of((1 - core) * h, 128), h)
    mine = pl.ds(pl.multiple_of(core * h, 128), h)
    pair = rcopy(pt.at[:, theirs], pair_in, pair_sem.at[0], pair_sem.at[1], at_replica(partner))
    pair.start()
    own_copies(0, start)
    z_pair = rcopy(zh.at[theirs], zh_in, zx_sem.at[0], zx_sem.at[1], at_replica(partner))
    z_pair.start()
    for hv in quarters:
        own_to_partner(hv).start()
    pair.wait_recv()
    total = pt[:, mine] + pair_in[...]
    half[...] = total
    half_bf[...] = total.astype(BF16)

    def rs_copies(act):
        for j in range(nc):
            target = first_owner + j

            @pl.when(pos != target)
            def _():
                act(rcopy(half_bf.at[:, pl.ds(j * w, w)], rs_in.at[pos], rs_send.at[j], rs_recv.at[pos],
                          at_replica(block_of(target))))

    rs_copies(start)
    for hv in quarters[1:-1]:
        own_copies(hv, start)

    owner = (pos >= first_owner) & (pos < first_owner + nc)
    own_index = jnp.clip(pos - first_owner, 0, nc - 1)

    def cols_of(cr, j):
        return pl.ds(pl.multiple_of(cr * h + j * w, 128), w)

    def fw_copy(cr, j):
        part = pm.at[:, cols_of(cr, j)]
        return rcopy(part, part, fw_send.at[j], ag_recv.at[cr, j], at_replica(partner))

    def ag_copy(k):
        part = pm.at[:, cols_of(core, own_index)]
        return rcopy(part, part, ag_send.at[k], ag_recv.at[core, own_index],
                     at_replica(block_of(lax.rem(pos + k, L))))

    tok_in.wait()
    a_buf[...] = dot(tok_v[...], base_v[...], NN)
    chip_block(pos)
    keys_of(pos)

    @pl.when(owner)
    def _():
        total = half[:, pl.ds(pl.multiple_of(own_index * w, 128), w)]
        for k in range(1, L):
            source = lax.rem(pos + k, L)
            rcopy(rs_in.at[source], rs_in.at[source], ag_send.at[k], rs_recv.at[source],
                  at_replica(partner)).wait_recv()
            total += rs_in[source].astype(F32)
        pm[:, cols_of(core, own_index)] = (total * (1.0 / R)).astype(BF16)
        for k in range(1, L):
            ag_copy(k).start()
        for j in range(nc):
            @pl.when(pos == first_owner + j)
            def _():
                fw_copy(core, j).start()

    own_copies(quarters[-1], start)
    z_pair.wait_recv()
    zs[...] = (zh[mine, :].astype(F32) + zh_in[...].astype(F32)).astype(BF16)
    arrived(1, *first)
    turn_of(pos)
    for j in range(nc):
        @pl.when(pos != first_owner + j)
        def _():
            fw_copy(core, j).wait_recv()
            fw_copy(core, j).start()

    tl[...] = dot(pm[:, mine], zs[...], NN)

    def tile_of(i):
        return (pl.ds(pl.multiple_of(lax.rem(i, groups) * 8, 8), 8),
                pl.ds(pl.multiple_of((i // groups) * wl, 128), wl))

    def if_owned(i, f):
        if tiles == plane:
            f()
        else:
            pl.when(i < tiles)(f)

    def t_copies(act):
        for k in range(1, plane):
            target = lax.rem(spot + k, plane)

            def go():
                a, b = tile_of(jnp.minimum(target, tiles - 1))
                act(rcopy(tl.at[a, b], t_in.at[spot], t_send.at[k], t_recv.at[spot], at_spot(target)))

            if_owned(target, go)

    t_copies(start)
    arrived(1, *second)
    for j in range(nc):
        fw_copy(1 - core, j).wait_recv()
    gs[...] = jnp.zeros_like(gs)
    gs[:, 0:rank] = dot(pm[...], pm[...], NT)

    def g_copy(k):
        return rcopy(gs, g_in.at[shard], g_send.at[k], g_recv.at[shard], at_shard(lax.rem(shard + k, S)))

    for k in range(1, S):
        g_copy(k).start()
    my_spot = jnp.minimum(spot, tiles - 1)
    my_rows, my_cols = tile_of(my_spot)

    def z_copy(k):
        part = z_in.at[pos]
        return rcopy(part, part, z_send.at[k], z_recv.at[pos], at_replica(block_of(lax.rem(pos + k, L))))

    def sum_plane():
        total = tl[my_rows, my_cols]
        for k in range(1, plane):
            source = lax.rem(spot + k, plane)
            rcopy(t_in.at[source], t_in.at[source], t_send.at[k], t_recv.at[source], at_replica(partner)).wait_recv()
            total += t_in[source]
        z_in[pos] = total
        for k in range(1, L):
            z_copy(k).start()

    if_owned(spot, sum_plane)
    bt[...] = dot(pm[...], tok_v[...], NT)

    def b_copy(k):
        target = lax.rem(shard + k, S)
        return rcopy(bt.at[:, token_rows(target)], b_in.at[shard], b_send.at[k], b_recv.at[shard], at_shard(target))

    for k in range(1, S):
        b_copy(k).start()
    arrived(2, *first)
    blocks_at(1, chip_block, keys_of)
    gram = gs[:, 0:rank]
    for k in range(1, S):
        source = lax.rem(shard + k, S)
        rcopy(g_in.at[source], g_in.at[source], g_send.at[k], g_recv.at[source], at_replica(partner)).wait_recv()
        gram = gram + g_in[source][:, 0:rank]
    inverse = invert(gram)

    def ta_copy(k):
        part = tt.at[my_rows, my_cols]
        return rcopy(part, part, ta_send.at[k], ta_recv.at[my_spot], at_spot(lax.rem(spot + k, plane)))

    def sum_planes():
        for k in range(1, L):
            source = lax.rem(pos + k, L)
            rcopy(z_in.at[source], z_in.at[source], z_send.at[k], z_recv.at[source], at_replica(partner)).wait_recv()
        total = z_in[0]
        for p in range(1, L):
            total += z_in[p]
        tt[my_rows, my_cols] = total * (1.0 / R)
        for k in range(1, plane):
            ta_copy(k).start()

    if_owned(spot, sum_planes)
    arrived(2, *second)
    blocks_at(1, turn_of)
    for step in range(2, L):
        if step > 2:
            arrived(step, *quarters)
        blocks_at(step, chip_block, keys_of, turn_of)
    if not early:
        def late(bk, carry):
            key_block(bk)
            turn_block(bk)
            return carry

        lax.fori_loop(0, blocks, late, 0)

    for k in range(1, plane):
        source = lax.rem(spot + k, plane)

        def got():
            i = jnp.minimum(source, tiles - 1)
            a, b = tile_of(i)
            rcopy(tt.at[a, b], tt.at[a, b], ta_send.at[k], ta_recv.at[i], at_replica(partner)).wait_recv()

        if_owned(source, got)
    x = lax.dot_general(inverse, tt[...], NN, precision=HIGHEST, preferred_element_type=F32)
    high, low = split2(x)
    x2[...] = jnp.concatenate([high, low], axis=0)
    pick = (lax.broadcasted_iota(jnp.int32, (kv, c), 0)
            == me * c + lax.broadcasted_iota(jnp.int32, (kv, c), 1)).astype(BF16)
    xo2[...] = dot(x2[...], pick, NN).astype(BF16)

    tile = min(256, d)

    def update_rows(t, carry):
        part = pl.ds(pl.multiple_of(t * tile, 128), tile)
        p = pm[:, part]
        p2 = jnp.concatenate([p, p], axis=0)
        u = dot(p2, x2[...], TN)
        ne_out[part, :] = (zf[part, :] - u).astype(BF16)
        nb_out[part, :] = (v_buf[part, :] - (outer_rate * (outer_mu + 1.0)) * u).astype(BF16)
        nm_out[:, part] = (outer_mu * slots[me, :, part].astype(F32) + dot(xo2[...], p2, TN)).astype(BF16)
        return carry

    lax.fori_loop(0, d // tile, update_rows, 0)

    b_total = bt[:, token_rows(shard)]
    for k in range(1, S):
        source = lax.rem(shard + k, S)
        rcopy(b_in.at[source], b_in.at[source], b_send.at[k], b_recv.at[source], at_replica(partner)).wait_recv()
        b_total += b_in[source]
    total = a_buf[token_rows(shard), :] - (outer_rate * (outer_mu + 1.0)) * lax.dot_general(
        b_total, x, TN, precision=HIGHEST, preferred_element_type=F32)
    for k in range(1, S):
        source = lax.rem(shard + k, S)
        for bk in range(blocks):
            part = a_in.at[source, :, block_cols(bk)]
            rcopy(part, part, a_send.at[k, bk], a_recv.at[source, bk], at_replica(partner)).wait_recv()
        total += a_in[source].astype(F32)
    key_out[...] = total.astype(BF16)

    for hv in range(HV):
        own_copies(hv, finish_send)
        own_to_partner(hv).wait_send()
        for step in range(1, L):
            passed_on(step, hv, finish_send, False)
    for k in range(1, S):
        for bk in range(blocks):
            a_copy(k, bk).wait_send()
        b_copy(k).wait_send()
        g_copy(k).wait_send()
    pair.wait_send()
    z_pair.wait_send()
    rs_copies(finish_send)
    t_copies(finish_send)
    for j in range(nc):
        fw_copy(core, j).wait_send()

    def drain_tile():
        for k in range(1, L):
            z_copy(k).wait_send()
        for k in range(1, plane):
            ta_copy(k).wait_send()

    if_owned(spot, drain_tile)

    @pl.when(owner)
    def _():
        for k in range(1, L):
            ag_copy(k).wait_send()


def store(nb, nm, ne, key, nb_out, nm_out, ne_out, key_out, sem):
    copies = [pltpu.make_async_copy(s, o, sem.at[i]) for i, (s, o) in
              enumerate(((nb, nb_out), (ne, ne_out), (nm, nm_out), (key, key_out)))]
    for cp in copies:
        cp.start()
    for cp in copies:
        cp.wait()


def on_device(local_weights, outer_base, momentum, error_feedback, q_start, tokens):
    R = lax.axis_size("replica")
    S = lax.axis_size("shard")
    d, kv = outer_base.shape
    rank = q_start.shape[1]
    c = momentum.shape[1]
    L = R // 2
    lw, ef, tok = local_weights[0], error_feedback[0], tokens[0]
    nt = tok.shape[0]
    n = nt // S
    blocks = kv // 128
    chunks = min(4, d // 128)
    h, nc, w, groups, tiles, wl = sizes(d, kv, rank, S)
    HV = HALVES
    V = pltpu.VMEM
    dma = pltpu.SemaphoreType.DMA
    hbm = pl.BlockSpec(memory_space=pltpu.HBM)
    anywhere = pl.BlockSpec(memory_space=pl.ANY)
    vm = pl.BlockSpec(memory_space=pltpu.VMEM)
    shapes = ((d, kv), (c, d), (d, kv), (n, kv))
    held = pl.pallas_call(
        functools.partial(exchange, (R, S, d, kv, rank)),
        out_shape=tuple(pltpu.VMEM(s, BF16) for s in shapes),
        in_specs=[hbm, hbm, hbm, vm, hbm, hbm],
        out_specs=(vm,) * 4,
        scratch_shapes=[
            V((d, kv), BF16), V((d, kv), BF16), V((d, kv), BF16), V((d, kv), BF16), V((h, kv), BF16), V((h, kv), BF16),
            V((d, kv), F32), V((nt, d), BF16), V((R, c, d), BF16), V((d, kv), F32),
            V((rank, d), F32), V((rank, h), F32), V((rank, h), F32), V((rank, h), BF16), V((L, rank, w), BF16),
            V((rank, d), BF16), V((rank, 128), F32), V((S, rank, 128), F32),
            V((rank, kv), F32), V((2 * S, 8, wl), F32), V((L, 8, wl), F32), V((rank, kv), F32),
            V((2 * rank, kv), BF16), V((2 * rank, c), BF16),
            V((nt, kv), F32), V((nt, kv), BF16), V((S, n, kv), BF16), V((rank, nt), F32), V((S, rank, n), F32),
            dma((3, chunks)), dma((2,)), dma((2,)), dma((2,)), dma((nc,)), dma((L,)), dma((L,)), dma((2, nc)), dma((nc,)),
            dma((S,)), dma((S,)), dma((2 * S,)), dma((2 * S,)), dma((L,)), dma((L,)), dma((2 * S,)), dma((tiles,)),
            dma((4, HV)), dma((2, L, HV)), dma((2, L, HV)), dma((R, HV)),
            dma((S, blocks)), dma((S, blocks)), dma((S,)), dma((S,)),
        ],
        compiler_params=pltpu.CompilerParams(collective_id=0, has_side_effects=True, vmem_limit_bytes=52 << 20),
        name="exchange",
    )(lw, outer_base, ef, q_start.T, momentum.T, tok)
    nb, nm, ne, keys = pl.pallas_call(
        store,
        out_shape=tuple(jax.ShapeDtypeStruct(s, BF16) for s in shapes),
        in_specs=[vm] * 4,
        out_specs=(anywhere,) * 4,
        scratch_shapes=[dma((4,))],
        compiler_params=pltpu.CompilerParams(vmem_limit_bytes=4 << 20),
        name="store",
    )(*held)
    return nb, nm.T, ne[None], keys[None]


def solution(mesh):
    in_specs = (
        P("replica", "shard", None),
        P("shard", None),
        P("shard", "replica"),
        P("replica", "shard", None),
        P(),
        P("replica", None, "shard"),
    )
    out_specs = (
        P("shard", None),
        P("shard", "replica"),
        P("replica", "shard", None),
        P("replica", "shard", None),
    )
    return jax.shard_map(
        on_device, mesh=mesh, in_specs=in_specs, out_specs=out_specs, check_vma=False
    )
```

```python
import functools

import jax
import jax.numpy as jnp
from jax import lax
from jax.experimental import pallas as pl
from jax.experimental.pallas import tpu as pltpu
from jax.sharding import PartitionSpec as P

outer_mu = 0.9
outer_rate = 0.7
MESH = pl.DeviceIdType.MESH
F32 = jnp.float32
BF16 = jnp.bfloat16
NT = (((1,), (1,)), ((), ()))
NN = (((1,), (0,)), ((), ()))
TN = (((0,), (0,)), ((), ()))
HIGHEST = lax.Precision.HIGHEST
HALVES = 4


def dot(a, b, dims):
    return lax.dot_general(a, b, dims, preferred_element_type=F32)


def split2(x):
    high = x.astype(BF16)
    return high, (x - high.astype(F32)).astype(BF16)


def invert(a):
    n = a.shape[0]
    rows = lax.broadcasted_iota(jnp.int32, (n, n), 0)
    cols = lax.broadcasted_iota(jnp.int32, (n, n), 1)
    lane = lax.broadcasted_iota(jnp.int32, (1, n), 1)
    for k in range(n):
        inverse_pivot = 1.0 / a[k : k + 1, k : k + 1]
        col = a[:, k : k + 1]
        row = jnp.where(lane == k, 1.0, a[k : k + 1, :]) * inverse_pivot
        a = jnp.where(rows == k, row, jnp.where(cols == k, 0.0, a) - col * row)
    return a


def sizes(d, kv, rank, S):
    h = d // 2
    nc = 2 if h % 256 == 0 else 1
    groups = rank // 8
    tiles = min(2 * S, groups * (kv // 128))
    return h, nc, h // nc, groups, tiles, kv // (tiles // groups)


def exchange(cfg, lw, base, ef, qt, mom, tok, nb_out, nm_out, ne_out, key_out,
             lw_v, base_v, ef_v, zh, zh_in, zs, zf, tok_v, slots, v_buf,
             pt, pair_in, half, half_bf, rs_in, pm, gs, g_in,
             tl, t_in, z_in, tt, x2, xo2, a_buf, a_bf, a_in, bt, b_in,
             ld_sem, mom_ld, pair_sem, zx_sem, rs_send, rs_recv, ag_send, ag_recv, fw_send,
             g_send, g_recv, t_send, t_recv, z_send, z_recv, ta_send, ta_recv,
             own_send, fz_send, fp_send, m_recv, a_send, a_recv, b_send, b_recv):
    R, S, d, kv, rank = cfg
    L = R // 2
    me = lax.axis_index("replica")
    shard = lax.axis_index("shard")
    core = lax.rem(me, 2)
    pos = me // 2
    partner = me + 1 - 2 * core
    chunks = ld_sem.shape[1]
    rows = d // chunks
    h, nc, w, groups, tiles, wl = sizes(d, kv, rank, S)
    first_owner = L // 2 - nc // 2
    c = slots.shape[1]
    per = 128 // c
    blocks = kv // 128
    n = tok_v.shape[0] // S
    early = per == 2
    HV = HALVES
    span = d // HV
    plane = 2 * S
    spot = 2 * shard + core

    def at_replica(r):
        return {"replica": r}

    def at_shard(s):
        return {"shard": s}

    def at_spot(i):
        return {"replica": 2 * pos + lax.rem(i, 2), "shard": i // 2}

    def block_of(p):
        return 2 * p + core

    def rcopy(src, dst, ss, rs, dev):
        return pltpu.make_async_remote_copy(src_ref=src, dst_ref=dst, send_sem=ss, recv_sem=rs,
                                            device_id=dev, device_id_type=MESH)

    barrier = pltpu.get_barrier_semaphore()
    for k in range(1, R):
        pl.semaphore_signal(barrier, inc=1, device_id=at_replica(lax.rem(me + k, R)), device_id_type=MESH)
    for k in range(1, S):
        for r in (me, partner):
            pl.semaphore_signal(barrier, inc=1, device_id={"replica": r, "shard": lax.rem(shard + k, S)},
                                device_id_type=MESH)

    loads = []
    for k in range(chunks):
        trio = []
        for i, (src, dst) in enumerate(((lw, lw_v), (base, base_v), (ef, ef_v))):
            part = pl.ds(k * rows, rows)
            cp = pltpu.make_async_copy(src.at[part], dst.at[part], ld_sem.at[i, k])
            cp.start()
            trio.append(cp)
        loads.append(trio)
    own_in = pltpu.make_async_copy(mom, slots.at[me], mom_ld.at[0])
    own_in.start()
    tok_in = pltpu.make_async_copy(tok, tok_v, mom_ld.at[1])
    tok_in.start()

    def slot(b, hv):
        return slots.at[b, :, pl.ds(hv * span, span)]

    def own_copy(i, hv, target):
        return rcopy(slot(me, hv), slot(me, hv), own_send.at[i, hv], m_recv.at[me, hv], at_replica(target))

    def own_near(act, *parts):
        def go(i, target):
            for hv in parts:
                act(own_copy(i, hv, target))

        @pl.when(pos + 1 < L)
        def _():
            go(0, block_of(jnp.minimum(pos + 1, L - 1)))

        @pl.when(pos >= 1)
        def _():
            go(1, block_of(jnp.maximum(pos - 1, 0)))

    def own_to_partner(hv):
        return own_copy(2, hv, partner)

    def start(cp):
        cp.start()

    def finish_send(cp):
        cp.wait_send()

    def await_half(b, hv):
        rcopy(slot(b, hv), slot(b, hv), own_send.at[0, hv], m_recv.at[b, hv], at_replica(partner)).wait_recv()

    def passed_on(step, hv, act, wait, relays=(True, False)):
        for side, sign in enumerate((-1, 1)):
            origin = pos + sign * step
            nxt = pos - sign
            inner = (nxt >= 0) & (nxt < L)
            there = (origin >= 0) & (origin < L)
            if relays == (True,):
                there = there & inner
            if relays == (False,):
                there = there & jnp.logical_not(inner)

            @pl.when(there)
            def _():
                b = block_of(jnp.clip(origin, 0, L - 1))
                if wait:
                    await_half(b, hv)
                here = inner
                @pl.when(here)
                def _():
                    act(rcopy(slot(b, hv), slot(b, hv), fz_send.at[side, step - 1, hv], m_recv.at[b, hv],
                              at_replica(block_of(jnp.clip(nxt, 0, L - 1)))))

                act(rcopy(slot(b, hv), slot(b, hv), fp_send.at[side, step - 1, hv], m_recv.at[b, hv],
                          at_replica(partner)))

    def arrived(step, *parts, relays=(True, False)):
        if step < L:
            for hv in parts:
                passed_on(step, hv, start, True, relays)

    def token_rows(s):
        return pl.ds(pl.multiple_of(s * n, 128), n)

    def block_cols(bk):
        return pl.ds(pl.multiple_of(bk * 128, 128), 128)

    def a_copy(k, bk):
        target = lax.rem(shard + k, S)
        return rcopy(a_bf.at[token_rows(target), block_cols(bk)], a_in.at[shard, :, block_cols(bk)],
                     a_send.at[k, bk], a_recv.at[shard, bk], at_shard(target))

    def key_block(bk):
        cols = block_cols(bk)
        block = slots[pl.ds(bk * per, per)].reshape(128, d)
        a = a_buf[:, cols] - (outer_rate * outer_mu * outer_mu) * dot(tok_v[...], block, NT)
        a_buf[:, cols] = a
        a_bf[:, cols] = a.astype(BF16)
        for k in range(1, S):
            a_copy(k, bk).start()

    def turn_block(bk):
        cols = block_cols(bk)
        turned = slots[pl.ds(bk * per, per)].reshape(128, d).T
        v_buf[:, cols] = base_v[:, cols].astype(F32) - (outer_rate * outer_mu * outer_mu) * turned.astype(F32)

    def chip_block(p):
        for hv in range(HV):
            await_half(2 * p + 1 - core, hv)

    def blocks_at(step, *fs):
        if not 0 < step < L:
            return

        def side(i, carry):
            origin = pos + (2 * i - 1) * step

            @pl.when((origin >= 0) & (origin < L))
            def _():
                for f in fs:
                    f(jnp.clip(origin, 0, L - 1))

            return carry

        lax.fori_loop(0, 2, side, 0)

    keys_of = key_block if early else lambda p: None
    turn_of = turn_block if early else lambda p: None
    quarters = tuple(range(HV))

    qh, ql = split2(qt[...])
    q2 = jnp.concatenate([qh, ql], axis=0)
    for k in range(chunks):
        for cp in loads[k]:
            cp.wait()
        part = pl.ds(k * rows, rows)
        z = base_v[part, :].astype(F32) - lw_v[part, :].astype(F32) + ef_v[part, :].astype(F32)
        zf[part, :] = z
        high, low = split2(z)
        zh[part, :] = high
        both = dot(q2, high, NT)
        pt[:, part] = both[:rank] + (both[rank:] + dot(qh, low, NT))

    own_in.wait()
    pl.semaphore_wait(barrier, R - 1 + 2 * (S - 1))

    theirs = pl.ds(pl.multiple_of((1 - core) * h, 128), h)
    mine = pl.ds(pl.multiple_of(core * h, 128), h)
    pair = rcopy(pt.at[:, theirs], pair_in, pair_sem.at[0], pair_sem.at[1], at_replica(partner))
    pair.start()
    own_near(start, 0)
    z_pair = rcopy(zh.at[theirs], zh_in, zx_sem.at[0], zx_sem.at[1], at_replica(partner))
    z_pair.start()
    for hv in quarters:
        own_to_partner(hv).start()
    pair.wait_recv()
    total = pt[:, mine] + pair_in[...]
    half[...] = total
    half_bf[...] = total.astype(BF16)

    def rs_copies(act):
        for j in range(nc):
            target = first_owner + j

            @pl.when(pos != target)
            def _():
                act(rcopy(half_bf.at[:, pl.ds(j * w, w)], rs_in.at[pos], rs_send.at[j], rs_recv.at[pos],
                          at_replica(block_of(target))))

    rs_copies(start)
    own_near(start, *quarters[1:])

    owner = (pos >= first_owner) & (pos < first_owner + nc)
    own_index = jnp.clip(pos - first_owner, 0, nc - 1)

    def cols_of(cr, j):
        return pl.ds(pl.multiple_of(cr * h + j * w, 128), w)

    def fw_copy(cr, j):
        part = pm.at[:, cols_of(cr, j)]
        return rcopy(part, part, fw_send.at[j], ag_recv.at[cr, j], at_replica(partner))

    def ag_copy(k):
        part = pm.at[:, cols_of(core, own_index)]
        return rcopy(part, part, ag_send.at[k], ag_recv.at[core, own_index],
                     at_replica(block_of(lax.rem(pos + k, L))))

    tok_in.wait()
    a_buf[...] = dot(tok_v[...], base_v[...], NN)
    chip_block(pos)
    keys_of(pos)

    @pl.when(owner)
    def _():
        total = half[:, pl.ds(pl.multiple_of(own_index * w, 128), w)]
        for k in range(1, L):
            source = lax.rem(pos + k, L)
            rcopy(rs_in.at[source], rs_in.at[source], ag_send.at[k], rs_recv.at[source],
                  at_replica(partner)).wait_recv()
            total += rs_in[source].astype(F32)
        pm[:, cols_of(core, own_index)] = (total * (1.0 / R)).astype(BF16)
        for k in range(1, L):
            ag_copy(k).start()
        for j in range(nc):
            @pl.when(pos == first_owner + j)
            def _():
                fw_copy(core, j).start()

    z_pair.wait_recv()
    zs[...] = (zh[mine, :].astype(F32) + zh_in[...].astype(F32)).astype(BF16)
    arrived(1, *quarters[:-2])
    turn_of(pos)
    arrived(1, quarters[-2])
    for j in range(nc):
        @pl.when(pos != first_owner + j)
        def _():
            fw_copy(core, j).wait_recv()
            fw_copy(core, j).start()

    tl[...] = dot(pm[:, mine], zs[...], NN)

    def tile_of(i):
        return (pl.ds(pl.multiple_of(lax.rem(i, groups) * 8, 8), 8),
                pl.ds(pl.multiple_of((i // groups) * wl, 128), wl))

    def if_owned(i, f):
        if tiles == plane:
            f()
        else:
            pl.when(i < tiles)(f)

    def t_copies(act):
        for k in range(1, plane):
            target = lax.rem(spot + k, plane)

            def go():
                a, b = tile_of(jnp.minimum(target, tiles - 1))
                act(rcopy(tl.at[a, b], t_in.at[spot], t_send.at[k], t_recv.at[spot], at_spot(target)))

            if_owned(target, go)

    t_copies(start)
    arrived(1, quarters[-1])
    arrived(2, quarters[0], relays=(True,))
    for j in range(nc):
        fw_copy(1 - core, j).wait_recv()
    gs[...] = jnp.zeros_like(gs)
    gs[:, 0:rank] = dot(pm[...], pm[...], NT)

    def g_copy(k):
        return rcopy(gs, g_in.at[shard], g_send.at[k], g_recv.at[shard], at_shard(lax.rem(shard + k, S)))

    for k in range(1, S):
        g_copy(k).start()
    my_spot = jnp.minimum(spot, tiles - 1)
    my_rows, my_cols = tile_of(my_spot)

    def z_copy(k):
        part = z_in.at[pos]
        return rcopy(part, part, z_send.at[k], z_recv.at[pos], at_replica(block_of(lax.rem(pos + k, L))))

    def sum_plane():
        total = tl[my_rows, my_cols]
        for k in range(1, plane):
            source = lax.rem(spot + k, plane)
            rcopy(t_in.at[source], t_in.at[source], t_send.at[k], t_recv.at[source], at_replica(partner)).wait_recv()
            total += t_in[source]
        z_in[pos] = total
        for k in range(1, L):
            z_copy(k).start()

    bt[...] = dot(pm[...], tok_v[...], NT)

    def b_copy(k):
        target = lax.rem(shard + k, S)
        return rcopy(bt.at[:, token_rows(target)], b_in.at[shard], b_send.at[k], b_recv.at[shard], at_shard(target))

    for k in range(1, S):
        b_copy(k).start()
    arrived(2, *quarters[1:-2], relays=(True,))
    if_owned(spot, sum_plane)
    arrived(2, *quarters[-2:], relays=(True,))
    arrived(2, quarters[0], relays=(False,))
    gram = gs[:, 0:rank]
    for k in range(1, S):
        source = lax.rem(shard + k, S)
        rcopy(g_in.at[source], g_in.at[source], g_send.at[k], g_recv.at[source], at_replica(partner)).wait_recv()
        gram = gram + g_in[source][:, 0:rank]
    inverse = invert(gram)
    blocks_at(1, chip_block, keys_of, turn_of)
    arrived(2, *quarters[1:-1], relays=(False,))

    def ta_copy(k):
        part = tt.at[my_rows, my_cols]
        return rcopy(part, part, ta_send.at[k], ta_recv.at[my_spot], at_spot(lax.rem(spot + k, plane)))

    def sum_planes():
        for k in range(1, L):
            source = lax.rem(pos + k, L)
            rcopy(z_in.at[source], z_in.at[source], z_send.at[k], z_recv.at[source], at_replica(partner)).wait_recv()
        total = z_in[0]
        for p in range(1, L):
            total += z_in[p]
        tt[my_rows, my_cols] = total * (1.0 / R)
        for k in range(1, plane):
            ta_copy(k).start()

    if_owned(spot, sum_planes)
    arrived(2, quarters[-1], relays=(False,))
    for step in range(2, L):
        if step > 2:
            arrived(step, *quarters)
        blocks_at(step, chip_block, keys_of, turn_of)
    if not early:
        def late(bk, carry):
            key_block(bk)
            turn_block(bk)
            return carry

        lax.fori_loop(0, blocks, late, 0)

    for k in range(1, plane):
        source = lax.rem(spot + k, plane)

        def got():
            i = jnp.minimum(source, tiles - 1)
            a, b = tile_of(i)
            rcopy(tt.at[a, b], tt.at[a, b], ta_send.at[k], ta_recv.at[i], at_replica(partner)).wait_recv()

        if_owned(source, got)
    x = lax.dot_general(inverse, tt[...], NN, precision=HIGHEST, preferred_element_type=F32)
    high, low = split2(x)
    x2[...] = jnp.concatenate([high, low], axis=0)
    pick = (lax.broadcasted_iota(jnp.int32, (kv, c), 0)
            == me * c + lax.broadcasted_iota(jnp.int32, (kv, c), 1)).astype(BF16)
    xo2[...] = dot(x2[...], pick, NN).astype(BF16)

    tile = min(256, d)

    def update_rows(t, carry):
        part = pl.ds(pl.multiple_of(t * tile, 128), tile)
        p = pm[:, part]
        p2 = jnp.concatenate([p, p], axis=0)
        u = dot(p2, x2[...], TN)
        ne_out[part, :] = (zf[part, :] - u).astype(BF16)
        nb_out[part, :] = (v_buf[part, :] - (outer_rate * (outer_mu + 1.0)) * u).astype(BF16)
        nm_out[:, part] = (outer_mu * slots[me, :, part].astype(F32) + dot(xo2[...], p2, TN)).astype(BF16)
        return carry

    lax.fori_loop(0, d // tile, update_rows, 0)

    b_total = bt[:, token_rows(shard)]
    for k in range(1, S):
        source = lax.rem(shard + k, S)
        rcopy(b_in.at[source], b_in.at[source], b_send.at[k], b_recv.at[source], at_replica(partner)).wait_recv()
        b_total += b_in[source]
    total = a_buf[token_rows(shard), :] - (outer_rate * (outer_mu + 1.0)) * lax.dot_general(
        b_total, x, TN, precision=HIGHEST, preferred_element_type=F32)
    for k in range(1, S):
        source = lax.rem(shard + k, S)
        for bk in range(blocks):
            part = a_in.at[source, :, block_cols(bk)]
            rcopy(part, part, a_send.at[k, bk], a_recv.at[source, bk], at_replica(partner)).wait_recv()
        total += a_in[source].astype(F32)
    key_out[...] = total.astype(BF16)

    own_near(finish_send, *quarters)
    for hv in quarters:
        own_to_partner(hv).wait_send()
        for step in range(1, L):
            passed_on(step, hv, finish_send, False)
    for k in range(1, S):
        for bk in range(blocks):
            a_copy(k, bk).wait_send()
        b_copy(k).wait_send()
        g_copy(k).wait_send()
    pair.wait_send()
    z_pair.wait_send()
    rs_copies(finish_send)
    t_copies(finish_send)
    for j in range(nc):
        fw_copy(core, j).wait_send()

    def drain_tile():
        for k in range(1, L):
            z_copy(k).wait_send()
        for k in range(1, plane):
            ta_copy(k).wait_send()

    if_owned(spot, drain_tile)

    @pl.when(owner)
    def _():
        for k in range(1, L):
            ag_copy(k).wait_send()


def store(nb, nm, ne, key, nb_out, nm_out, ne_out, key_out, sem):
    copies = [pltpu.make_async_copy(s, o, sem.at[i]) for i, (s, o) in
              enumerate(((nb, nb_out), (ne, ne_out), (nm, nm_out), (key, key_out)))]
    for cp in copies:
        cp.start()
    for cp in copies:
        cp.wait()


def on_device(local_weights, outer_base, momentum, error_feedback, q_start, tokens):
    R = lax.axis_size("replica")
    S = lax.axis_size("shard")
    d, kv = outer_base.shape
    rank = q_start.shape[1]
    c = momentum.shape[1]
    L = R // 2
    lw, ef, tok = local_weights[0], error_feedback[0], tokens[0]
    nt = tok.shape[0]
    n = nt // S
    blocks = kv // 128
    chunks = min(4, d // 128)
    h, nc, w, groups, tiles, wl = sizes(d, kv, rank, S)
    HV = HALVES
    V = pltpu.VMEM
    dma = pltpu.SemaphoreType.DMA
    hbm = pl.BlockSpec(memory_space=pltpu.HBM)
    anywhere = pl.BlockSpec(memory_space=pl.ANY)
    vm = pl.BlockSpec(memory_space=pltpu.VMEM)
    shapes = ((d, kv), (c, d), (d, kv), (n, kv))
    held = pl.pallas_call(
        functools.partial(exchange, (R, S, d, kv, rank)),
        out_shape=tuple(pltpu.VMEM(s, BF16) for s in shapes),
        in_specs=[hbm, hbm, hbm, vm, hbm, hbm],
        out_specs=(vm,) * 4,
        scratch_shapes=[
            V((d, kv), BF16), V((d, kv), BF16), V((d, kv), BF16), V((d, kv), BF16), V((h, kv), BF16), V((h, kv), BF16),
            V((d, kv), F32), V((nt, d), BF16), V((R, c, d), BF16), V((d, kv), F32),
            V((rank, d), F32), V((rank, h), F32), V((rank, h), F32), V((rank, h), BF16), V((L, rank, w), BF16),
            V((rank, d), BF16), V((rank, 128), F32), V((S, rank, 128), F32),
            V((rank, kv), F32), V((2 * S, 8, wl), F32), V((L, 8, wl), F32), V((rank, kv), F32),
            V((2 * rank, kv), BF16), V((2 * rank, c), BF16),
            V((nt, kv), F32), V((nt, kv), BF16), V((S, n, kv), BF16), V((rank, nt), F32), V((S, rank, n), F32),
            dma((3, chunks)), dma((2,)), dma((2,)), dma((2,)), dma((nc,)), dma((L,)), dma((L,)), dma((2, nc)), dma((nc,)),
            dma((S,)), dma((S,)), dma((2 * S,)), dma((2 * S,)), dma((L,)), dma((L,)), dma((2 * S,)), dma((tiles,)),
            dma((4, HV)), dma((2, L, HV)), dma((2, L, HV)), dma((R, HV)),
            dma((S, blocks)), dma((S, blocks)), dma((S,)), dma((S,)),
        ],
        compiler_params=pltpu.CompilerParams(collective_id=0, has_side_effects=True, vmem_limit_bytes=52 << 20),
        name="exchange",
    )(lw, outer_base, ef, q_start.T, momentum.T, tok)
    nb, nm, ne, keys = pl.pallas_call(
        store,
        out_shape=tuple(jax.ShapeDtypeStruct(s, BF16) for s in shapes),
        in_specs=[vm] * 4,
        out_specs=(anywhere,) * 4,
        scratch_shapes=[dma((4,))],
        compiler_params=pltpu.CompilerParams(vmem_limit_bytes=4 << 20),
        name="store",
    )(*held)
    return nb, nm.T, ne[None], keys[None]


def solution(mesh):
    in_specs = (
        P("replica", "shard", None),
        P("shard", None),
        P("shard", "replica"),
        P("replica", "shard", None),
        P(),
        P("replica", None, "shard"),
    )
    out_specs = (
        P("shard", None),
        P("shard", "replica"),
        P("replica", "shard", None),
        P("replica", "shard", None),
    )
    return jax.shard_map(
        on_device, mesh=mesh, in_specs=in_specs, out_specs=out_specs, check_vma=False
    )
```

```python
import functools

import jax
import jax.numpy as jnp
from jax import lax
from jax.experimental import pallas as pl
from jax.experimental.pallas import tpu as pltpu
from jax.sharding import PartitionSpec as P

outer_mu = 0.9
outer_rate = 0.7
MESH = pl.DeviceIdType.MESH
F32 = jnp.float32
BF16 = jnp.bfloat16
NT = (((1,), (1,)), ((), ()))
NN = (((1,), (0,)), ((), ()))
TN = (((0,), (0,)), ((), ()))
HIGHEST = lax.Precision.HIGHEST
HALVES = 4


def dot(a, b, dims):
    return lax.dot_general(a, b, dims, preferred_element_type=F32)


def split2(x):
    high = x.astype(BF16)
    return high, (x - high.astype(F32)).astype(BF16)


def invert(a):
    n = a.shape[0]
    rows = lax.broadcasted_iota(jnp.int32, (n, n), 0)
    cols = lax.broadcasted_iota(jnp.int32, (n, n), 1)
    lane = lax.broadcasted_iota(jnp.int32, (1, n), 1)
    for k in range(n):
        inverse_pivot = 1.0 / a[k : k + 1, k : k + 1]
        col = a[:, k : k + 1]
        row = jnp.where(lane == k, 1.0, a[k : k + 1, :]) * inverse_pivot
        a = jnp.where(rows == k, row, jnp.where(cols == k, 0.0, a) - col * row)
    return a


def sizes(d, kv, rank, S):
    h = d // 2
    nc = 2 if h % 256 == 0 else 1
    groups = rank // 8
    tiles = min(2 * S, groups * (kv // 128))
    return h, nc, h // nc, groups, tiles, kv // (tiles // groups)


def exchange(cfg, lw, base, ef, qt, mom, tok, pm, x2, xo2, zf, v_buf, own_out, key_out,
             lw_v, base_v, ef_v, zh, zh_in, zs, tok_v, slots, pick,
             pt, pair_in, half, half_bf, rs_in, gs, g_in,
             tl, t_in, z_in, tt, a_buf, a_bf, a_in, bt, b_in,
             ld_sem, mom_ld, pair_sem, zx_sem, rs_send, rs_recv, ag_send, ag_recv, fw_send,
             g_send, g_recv, t_send, t_recv, z_send, z_recv, ta_send, ta_recv,
             own_send, fz_send, fp_send, m_recv, a_send, a_recv, b_send, b_recv):
    R, S, d, kv, rank = cfg
    L = R // 2
    me = lax.axis_index("replica")
    shard = lax.axis_index("shard")
    core = lax.rem(me, 2)
    pos = me // 2
    partner = me + 1 - 2 * core
    chunks = ld_sem.shape[1]
    rows = d // chunks
    h, nc, w, groups, tiles, wl = sizes(d, kv, rank, S)
    first_owner = L // 2 - nc // 2
    c = slots.shape[1]
    per = 128 // c
    blocks = kv // 128
    n = tok_v.shape[0] // S
    early = per == 2
    HV = HALVES
    span = d // HV
    plane = 2 * S
    spot = 2 * shard + core

    def at_replica(r):
        return {"replica": r}

    def at_shard(s):
        return {"shard": s}

    def at_spot(i):
        return {"replica": 2 * pos + lax.rem(i, 2), "shard": i // 2}

    def block_of(p):
        return 2 * p + core

    def rcopy(src, dst, ss, rs, dev):
        return pltpu.make_async_remote_copy(src_ref=src, dst_ref=dst, send_sem=ss, recv_sem=rs,
                                            device_id=dev, device_id_type=MESH)

    barrier = pltpu.get_barrier_semaphore()
    for k in range(1, R):
        pl.semaphore_signal(barrier, inc=1, device_id=at_replica(lax.rem(me + k, R)), device_id_type=MESH)
    for k in range(1, S):
        for r in (me, partner):
            pl.semaphore_signal(barrier, inc=1, device_id={"replica": r, "shard": lax.rem(shard + k, S)},
                                device_id_type=MESH)

    loads = []
    for k in range(chunks):
        trio = []
        for i, (src, dst) in enumerate(((lw, lw_v), (base, base_v), (ef, ef_v))):
            part = pl.ds(k * rows, rows)
            cp = pltpu.make_async_copy(src.at[part], dst.at[part], ld_sem.at[i, k])
            cp.start()
            trio.append(cp)
        loads.append(trio)
    own_in = pltpu.make_async_copy(mom, slots.at[me], mom_ld.at[0])
    own_in.start()
    tok_in = pltpu.make_async_copy(tok, tok_v, mom_ld.at[1])
    tok_in.start()

    def slot(b, hv):
        return slots.at[b, :, pl.ds(hv * span, span)]

    def own_copy(i, hv, target):
        return rcopy(slot(me, hv), slot(me, hv), own_send.at[i, hv], m_recv.at[me, hv], at_replica(target))

    def own_near(act, *parts):
        def go(i, target):
            for hv in parts:
                act(own_copy(i, hv, target))

        @pl.when(pos + 1 < L)
        def _():
            go(0, block_of(jnp.minimum(pos + 1, L - 1)))

        @pl.when(pos >= 1)
        def _():
            go(1, block_of(jnp.maximum(pos - 1, 0)))

    def own_to_partner(hv):
        return own_copy(2, hv, partner)

    def start(cp):
        cp.start()

    def finish_send(cp):
        cp.wait_send()

    def await_half(b, hv):
        rcopy(slot(b, hv), slot(b, hv), own_send.at[0, hv], m_recv.at[b, hv], at_replica(partner)).wait_recv()

    def passed_on(step, hv, act, wait, relays=(True, False)):
        for side, sign in enumerate((-1, 1)):
            origin = pos + sign * step
            nxt = pos - sign
            inner = (nxt >= 0) & (nxt < L)
            there = (origin >= 0) & (origin < L)
            if relays == (True,):
                there = there & inner
            if relays == (False,):
                there = there & jnp.logical_not(inner)

            @pl.when(there)
            def _():
                b = block_of(jnp.clip(origin, 0, L - 1))
                if wait:
                    await_half(b, hv)
                here = inner
                @pl.when(here)
                def _():
                    act(rcopy(slot(b, hv), slot(b, hv), fz_send.at[side, step - 1, hv], m_recv.at[b, hv],
                              at_replica(block_of(jnp.clip(nxt, 0, L - 1)))))

                act(rcopy(slot(b, hv), slot(b, hv), fp_send.at[side, step - 1, hv], m_recv.at[b, hv],
                          at_replica(partner)))

    def arrived(step, *parts, relays=(True, False)):
        if step < L:
            for hv in parts:
                passed_on(step, hv, start, True, relays)

    def token_rows(s):
        return pl.ds(pl.multiple_of(s * n, 128), n)

    def block_cols(bk):
        return pl.ds(pl.multiple_of(bk * 128, 128), 128)

    def a_copy(k, bk):
        target = lax.rem(shard + k, S)
        return rcopy(a_bf.at[token_rows(target), block_cols(bk)], a_in.at[shard, :, block_cols(bk)],
                     a_send.at[k, bk], a_recv.at[shard, bk], at_shard(target))

    def key_block(bk):
        cols = block_cols(bk)
        block = slots[pl.ds(bk * per, per)].reshape(128, d)
        a = a_buf[:, cols] - (outer_rate * outer_mu * outer_mu) * dot(tok_v[...], block, NT)
        a_buf[:, cols] = a
        a_bf[:, cols] = a.astype(BF16)
        for k in range(1, S):
            a_copy(k, bk).start()

    def turn_block(bk):
        cols = block_cols(bk)
        turned = slots[pl.ds(bk * per, per)].reshape(128, d).T
        v_buf[:, cols] = base_v[:, cols].astype(F32) - (outer_rate * outer_mu * outer_mu) * turned.astype(F32)

    def chip_block(p):
        for hv in range(HV):
            await_half(2 * p + 1 - core, hv)

    def blocks_at(step, *fs):
        if not 0 < step < L:
            return

        def side(i, carry):
            origin = pos + (2 * i - 1) * step

            @pl.when((origin >= 0) & (origin < L))
            def _():
                for f in fs:
                    f(jnp.clip(origin, 0, L - 1))

            return carry

        lax.fori_loop(0, 2, side, 0)

    keys_of = key_block if early else lambda p: None
    turn_of = turn_block if early else lambda p: None
    quarters = tuple(range(HV))

    qh, ql = split2(qt[...])
    q2 = jnp.concatenate([qh, ql], axis=0)
    for k in range(chunks):
        for cp in loads[k]:
            cp.wait()
        part = pl.ds(k * rows, rows)
        z = base_v[part, :].astype(F32) - lw_v[part, :].astype(F32) + ef_v[part, :].astype(F32)
        zf[part, :] = z
        high, low = split2(z)
        zh[part, :] = high
        both = dot(q2, high, NT)
        pt[:, part] = both[:rank] + (both[rank:] + dot(qh, low, NT))

    own_in.wait()
    pl.semaphore_wait(barrier, R - 1 + 2 * (S - 1))

    theirs = pl.ds(pl.multiple_of((1 - core) * h, 128), h)
    mine = pl.ds(pl.multiple_of(core * h, 128), h)
    pair = rcopy(pt.at[:, theirs], pair_in, pair_sem.at[0], pair_sem.at[1], at_replica(partner))
    pair.start()
    own_near(start, 0)
    z_pair = rcopy(zh.at[theirs], zh_in, zx_sem.at[0], zx_sem.at[1], at_replica(partner))
    z_pair.start()
    for hv in quarters:
        own_to_partner(hv).start()
    pair.wait_recv()
    total = pt[:, mine] + pair_in[...]
    half[...] = total
    half_bf[...] = total.astype(BF16)

    def rs_copies(act):
        for j in range(nc):
            target = first_owner + j

            @pl.when(pos != target)
            def _():
                act(rcopy(half_bf.at[:, pl.ds(j * w, w)], rs_in.at[pos], rs_send.at[j], rs_recv.at[pos],
                          at_replica(block_of(target))))

    rs_copies(start)
    own_near(start, *quarters[1:])

    owner = (pos >= first_owner) & (pos < first_owner + nc)
    own_index = jnp.clip(pos - first_owner, 0, nc - 1)

    def cols_of(cr, j):
        return pl.ds(pl.multiple_of(cr * h + j * w, 128), w)

    def fw_copy(cr, j):
        part = pm.at[:, cols_of(cr, j)]
        return rcopy(part, part, fw_send.at[j], ag_recv.at[cr, j], at_replica(partner))

    def ag_copy(k):
        part = pm.at[:, cols_of(core, own_index)]
        return rcopy(part, part, ag_send.at[k], ag_recv.at[core, own_index],
                     at_replica(block_of(lax.rem(pos + k, L))))

    tok_in.wait()
    a_buf[...] = dot(tok_v[...], base_v[...], NN)
    chip_block(pos)
    keys_of(pos)

    @pl.when(owner)
    def _():
        total = half[:, pl.ds(pl.multiple_of(own_index * w, 128), w)]
        for k in range(1, L):
            source = lax.rem(pos + k, L)
            rcopy(rs_in.at[source], rs_in.at[source], ag_send.at[k], rs_recv.at[source],
                  at_replica(partner)).wait_recv()
            total += rs_in[source].astype(F32)
        pm[:, cols_of(core, own_index)] = (total * (1.0 / R)).astype(BF16)
        for k in range(1, L):
            ag_copy(k).start()
        for j in range(nc):
            @pl.when(pos == first_owner + j)
            def _():
                fw_copy(core, j).start()

    z_pair.wait_recv()
    zs[...] = (zh[mine, :].astype(F32) + zh_in[...].astype(F32)).astype(BF16)
    arrived(1, *quarters[:-2])
    turn_of(pos)
    own_out[...] = slots[me]
    pick[...] = (lax.broadcasted_iota(jnp.int32, (kv, c), 0)
                 == me * c + lax.broadcasted_iota(jnp.int32, (kv, c), 1)).astype(BF16)
    arrived(1, quarters[-2])
    for j in range(nc):
        @pl.when(pos != first_owner + j)
        def _():
            fw_copy(core, j).wait_recv()
            fw_copy(core, j).start()

    tl[...] = dot(pm[:, mine], zs[...], NN)

    def tile_of(i):
        return (pl.ds(pl.multiple_of(lax.rem(i, groups) * 8, 8), 8),
                pl.ds(pl.multiple_of((i // groups) * wl, 128), wl))

    def if_owned(i, f):
        if tiles == plane:
            f()
        else:
            pl.when(i < tiles)(f)

    def t_copies(act):
        for k in range(1, plane):
            target = lax.rem(spot + k, plane)

            def go():
                a, b = tile_of(jnp.minimum(target, tiles - 1))
                act(rcopy(tl.at[a, b], t_in.at[spot], t_send.at[k], t_recv.at[spot], at_spot(target)))

            if_owned(target, go)

    t_copies(start)
    arrived(1, quarters[-1])
    arrived(2, quarters[0], relays=(True,))
    for j in range(nc):
        fw_copy(1 - core, j).wait_recv()
    gs[...] = jnp.zeros_like(gs)
    gs[:, 0:rank] = dot(pm[...], pm[...], NT)

    def g_copy(k):
        return rcopy(gs, g_in.at[shard], g_send.at[k], g_recv.at[shard], at_shard(lax.rem(shard + k, S)))

    for k in range(1, S):
        g_copy(k).start()
    my_spot = jnp.minimum(spot, tiles - 1)
    my_rows, my_cols = tile_of(my_spot)

    def z_copy(k):
        part = z_in.at[pos]
        return rcopy(part, part, z_send.at[k], z_recv.at[pos], at_replica(block_of(lax.rem(pos + k, L))))

    def sum_plane():
        total = tl[my_rows, my_cols]
        for k in range(1, plane):
            source = lax.rem(spot + k, plane)
            rcopy(t_in.at[source], t_in.at[source], t_send.at[k], t_recv.at[source], at_replica(partner)).wait_recv()
            total += t_in[source]
        z_in[pos] = total
        for k in range(1, L):
            z_copy(k).start()

    bt[...] = dot(pm[...], tok_v[...], NT)

    def b_copy(k):
        target = lax.rem(shard + k, S)
        return rcopy(bt.at[:, token_rows(target)], b_in.at[shard], b_send.at[k], b_recv.at[shard], at_shard(target))

    for k in range(1, S):
        b_copy(k).start()
    arrived(2, *quarters[1:-2], relays=(True,))
    if_owned(spot, sum_plane)
    arrived(2, *quarters[-2:], relays=(True,))
    arrived(2, quarters[0], relays=(False,))
    gram = gs[:, 0:rank]
    for k in range(1, S):
        source = lax.rem(shard + k, S)
        rcopy(g_in.at[source], g_in.at[source], g_send.at[k], g_recv.at[source], at_replica(partner)).wait_recv()
        gram = gram + g_in[source][:, 0:rank]
    inverse = invert(gram)
    blocks_at(1, chip_block, keys_of, turn_of)
    arrived(2, *quarters[1:-1], relays=(False,))

    def ta_copy(k):
        part = tt.at[my_rows, my_cols]
        return rcopy(part, part, ta_send.at[k], ta_recv.at[my_spot], at_spot(lax.rem(spot + k, plane)))

    def sum_planes():
        for k in range(1, L):
            source = lax.rem(pos + k, L)
            rcopy(z_in.at[source], z_in.at[source], z_send.at[k], z_recv.at[source], at_replica(partner)).wait_recv()
        total = z_in[0]
        for p in range(1, L):
            total += z_in[p]
        tt[my_rows, my_cols] = total * (1.0 / R)
        for k in range(1, plane):
            ta_copy(k).start()

    if_owned(spot, sum_planes)
    arrived(2, quarters[-1], relays=(False,))
    for step in range(2, L):
        if step > 2:
            arrived(step, *quarters)
        blocks_at(step, chip_block, keys_of, turn_of)
    if not early:
        def late(bk, carry):
            key_block(bk)
            turn_block(bk)
            return carry

        lax.fori_loop(0, blocks, late, 0)

    pair.wait_send()
    z_pair.wait_send()
    rs_copies(finish_send)
    t_copies(finish_send)
    own_near(finish_send, *quarters)
    for hv in quarters:
        own_to_partner(hv).wait_send()
    for k in range(1, S):
        b_copy(k).wait_send()
        g_copy(k).wait_send()
    for j in range(nc):
        fw_copy(core, j).wait_send()

    def drain_z():
        for k in range(1, L):
            z_copy(k).wait_send()

    if_owned(spot, drain_z)

    @pl.when(owner)
    def _():
        for k in range(1, L):
            ag_copy(k).wait_send()

    for k in range(1, plane):
        source = lax.rem(spot + k, plane)

        def got():
            i = jnp.minimum(source, tiles - 1)
            a, b = tile_of(i)
            rcopy(tt.at[a, b], tt.at[a, b], ta_send.at[k], ta_recv.at[i], at_replica(partner)).wait_recv()

        if_owned(source, got)
    x = lax.dot_general(inverse, tt[...], NN, precision=HIGHEST, preferred_element_type=F32)
    high, low = split2(x)
    x2[...] = jnp.concatenate([high, low], axis=0)
    xo2[...] = dot(x2[...], pick[...], NN).astype(BF16)

    b_total = bt[:, token_rows(shard)]
    for k in range(1, S):
        source = lax.rem(shard + k, S)
        rcopy(b_in.at[source], b_in.at[source], b_send.at[k], b_recv.at[source], at_replica(partner)).wait_recv()
        b_total += b_in[source]
    total = a_buf[token_rows(shard), :] - (outer_rate * (outer_mu + 1.0)) * lax.dot_general(
        b_total, x, TN, precision=HIGHEST, preferred_element_type=F32)
    for hv in quarters:
        for step in range(1, L):
            passed_on(step, hv, finish_send, False)
    for k in range(1, S):
        source = lax.rem(shard + k, S)
        for bk in range(blocks):
            part = a_in.at[source, :, block_cols(bk)]
            rcopy(part, part, a_send.at[k, bk], a_recv.at[source, bk], at_replica(partner)).wait_recv()
        total += a_in[source].astype(F32)
    key_out[...] = total.astype(BF16)

    for k in range(1, S):
        for bk in range(blocks):
            a_copy(k, bk).wait_send()

    def drain_tile():
        for k in range(1, plane):
            ta_copy(k).wait_send()

    if_owned(spot, drain_tile)


def update_rows(pm, x2, xo2, zf, v, own, key, nb_out, nm_out, ne_out, key_out, nb, nm, ne, sem, rest):
    d = zf.shape[0]
    tile = min(256, d)
    copies = [pltpu.make_async_copy(key, key_out, rest.at[0])]
    copies[0].start()
    for t in range(d // tile):
        part = pl.ds(t * tile, tile)
        p = pm[:, part]
        p2 = jnp.concatenate([p, p], axis=0)
        u = dot(p2, x2[...], TN)
        ne[part, :] = (zf[part, :] - u).astype(BF16)
        nb[part, :] = (v[part, :] - (outer_rate * (outer_mu + 1.0)) * u).astype(BF16)
        for i, (held, out) in enumerate(((ne, ne_out), (nb, nb_out))):
            cp = pltpu.make_async_copy(held.at[part], out.at[part], sem.at[i, t])
            cp.start()
            copies.append(cp)
        if t == 0:
            whole = pm[...]
            nm[...] = (outer_mu * own[...].astype(F32)
                       + dot(xo2[...], jnp.concatenate([whole, whole], axis=0), TN)).astype(BF16)
            cp = pltpu.make_async_copy(nm, nm_out, rest.at[1])
            cp.start()
            copies.append(cp)
    for cp in copies:
        cp.wait()


def on_device(local_weights, outer_base, momentum, error_feedback, q_start, tokens):
    R = lax.axis_size("replica")
    S = lax.axis_size("shard")
    d, kv = outer_base.shape
    rank = q_start.shape[1]
    c = momentum.shape[1]
    L = R // 2
    lw, ef, tok = local_weights[0], error_feedback[0], tokens[0]
    nt = tok.shape[0]
    n = nt // S
    blocks = kv // 128
    chunks = min(4, d // 128)
    h, nc, w, groups, tiles, wl = sizes(d, kv, rank, S)
    HV = HALVES
    V = pltpu.VMEM
    dma = pltpu.SemaphoreType.DMA
    hbm = pl.BlockSpec(memory_space=pltpu.HBM)
    anywhere = pl.BlockSpec(memory_space=pl.ANY)
    vm = pl.BlockSpec(memory_space=pltpu.VMEM)
    shapes = ((d, kv), (c, d), (d, kv), (n, kv))
    tiles_out = d // min(256, d)
    passed = ((rank, d), BF16), ((2 * rank, kv), BF16), ((2 * rank, c), BF16), ((d, kv), F32), ((d, kv), F32), ((c, d), BF16), ((n, kv), BF16)
    held = pl.pallas_call(
        functools.partial(exchange, (R, S, d, kv, rank)),
        out_shape=tuple(pltpu.VMEM(s, t) for s, t in passed),
        in_specs=[hbm, hbm, hbm, vm, hbm, hbm],
        out_specs=(vm,) * len(passed),
        scratch_shapes=[
            V((d, kv), BF16), V((d, kv), BF16), V((d, kv), BF16), V((d, kv), BF16), V((h, kv), BF16), V((h, kv), BF16),
            V((nt, d), BF16), V((R, c, d), BF16), V((kv, c), BF16),
            V((rank, d), F32), V((rank, h), F32), V((rank, h), F32), V((rank, h), BF16), V((L, rank, w), BF16),
            V((rank, 128), F32), V((S, rank, 128), F32),
            V((rank, kv), F32), V((2 * S, 8, wl), F32), V((L, 8, wl), F32), V((rank, kv), F32),
            V((nt, kv), F32), V((nt, kv), BF16), V((S, n, kv), BF16), V((rank, nt), F32), V((S, rank, n), F32),
            dma((3, chunks)), dma((2,)), dma((2,)), dma((2,)), dma((nc,)), dma((L,)), dma((L,)), dma((2, nc)), dma((nc,)),
            dma((S,)), dma((S,)), dma((2 * S,)), dma((2 * S,)), dma((L,)), dma((L,)), dma((2 * S,)), dma((tiles,)),
            dma((4, HV)), dma((2, L, HV)), dma((2, L, HV)), dma((R, HV)),
            dma((S, blocks)), dma((S, blocks)), dma((S,)), dma((S,)),
        ],
        compiler_params=pltpu.CompilerParams(collective_id=0, has_side_effects=True, vmem_limit_bytes=48 << 20),
        name="exchange",
    )(lw, outer_base, ef, q_start.T, momentum.T, tok)
    nb, nm, ne, keys = pl.pallas_call(
        update_rows,
        out_shape=tuple(jax.ShapeDtypeStruct(s, BF16) for s in shapes),
        in_specs=[vm] * len(passed),
        out_specs=(anywhere,) * 4,
        scratch_shapes=[V(s, BF16) for s in shapes[:3]] + [dma((2, tiles_out)), dma((2,))],
        compiler_params=pltpu.CompilerParams(vmem_limit_bytes=16 << 20),
        name="update_rows",
    )(*held)
    return nb, nm.T, ne[None], keys[None]


def solution(mesh):
    in_specs = (
        P("replica", "shard", None),
        P("shard", None),
        P("shard", "replica"),
        P("replica", "shard", None),
        P(),
        P("replica", None, "shard"),
    )
    out_specs = (
        P("shard", None),
        P("shard", "replica"),
        P("replica", "shard", None),
        P("replica", "shard", None),
    )
    return jax.shard_map(
        on_device, mesh=mesh, in_specs=in_specs, out_specs=out_specs, check_vma=False
    )
```

```python
import functools

import jax
import jax.numpy as jnp
from jax import lax
from jax.experimental import pallas as pl
from jax.experimental.pallas import tpu as pltpu
from jax.sharding import PartitionSpec as P

outer_mu = 0.9
outer_rate = 0.7
MESH = pl.DeviceIdType.MESH
F32 = jnp.float32
BF16 = jnp.bfloat16
NT = (((1,), (1,)), ((), ()))
NN = (((1,), (0,)), ((), ()))
TN = (((0,), (0,)), ((), ()))
HIGHEST = lax.Precision.HIGHEST
HALVES = 4


def dot(a, b, dims):
    return lax.dot_general(a, b, dims, preferred_element_type=F32)


def split2(x):
    high = x.astype(BF16)
    return high, (x - high.astype(F32)).astype(BF16)


def invert(a):
    n = a.shape[0]
    rows = lax.broadcasted_iota(jnp.int32, (n, n), 0)
    cols = lax.broadcasted_iota(jnp.int32, (n, n), 1)
    lane = lax.broadcasted_iota(jnp.int32, (1, n), 1)
    for k in range(n):
        inverse_pivot = 1.0 / a[k : k + 1, k : k + 1]
        col = a[:, k : k + 1]
        row = jnp.where(lane == k, 1.0, a[k : k + 1, :]) * inverse_pivot
        a = jnp.where(rows == k, row, jnp.where(cols == k, 0.0, a) - col * row)
    return a


def sizes(d, kv, rank, S):
    h = d // 2
    nc = 2 if h % 256 == 0 else 1
    groups = rank // 8
    tiles = min(2 * S, groups * (kv // 128))
    return h, nc, h // nc, groups, tiles, kv // (tiles // groups)


def exchange(cfg, lw, base, ef, qt, mom, tok, pm, x2, xo2, zf, v_buf, own_out, key_out,
             lw_v, base_v, ef_v, zh, zh_in, zs, tok_v, slots, pick,
             pt, pair_in, half, half_bf, rs_in, gs, g_in,
             tl, t_in, z_in, tt, a_buf, a_bf, a_in, bt, b_in,
             ld_sem, mom_ld, pair_sem, zx_sem, rs_send, rs_recv, ag_send, ag_recv, fw_send,
             g_send, g_recv, t_send, t_recv, z_send, z_recv, ta_send, ta_recv,
             own_send, fz_send, fp_send, m_recv, a_send, a_recv, b_send, b_recv):
    R, S, d, kv, rank = cfg
    L = R // 2
    me = lax.axis_index("replica")
    shard = lax.axis_index("shard")
    core = lax.rem(me, 2)
    pos = me // 2
    partner = me + 1 - 2 * core
    chunks = ld_sem.shape[1]
    rows = d // chunks
    h, nc, w, groups, tiles, wl = sizes(d, kv, rank, S)
    first_owner = L // 2 - nc // 2
    c = slots.shape[1]
    per = 128 // c
    blocks = kv // 128
    n = tok_v.shape[0] // S
    early = per == 2
    HV = HALVES
    span = d // HV
    plane = 2 * S
    spot = 2 * shard + core

    def at_replica(r):
        return {"replica": r}

    def at_shard(s):
        return {"shard": s}

    def at_spot(i):
        return {"replica": 2 * pos + lax.rem(i, 2), "shard": i // 2}

    def block_of(p):
        return 2 * p + core

    def rcopy(src, dst, ss, rs, dev):
        return pltpu.make_async_remote_copy(src_ref=src, dst_ref=dst, send_sem=ss, recv_sem=rs,
                                            device_id=dev, device_id_type=MESH)

    barrier = pltpu.get_barrier_semaphore()
    pl.semaphore_signal(barrier, inc=1, device_id=at_replica(partner), device_id_type=MESH)
    for k in range(1, L):
        pl.semaphore_signal(barrier, inc=1, device_id=at_replica(block_of(lax.rem(pos + k, L))), device_id_type=MESH)
    for k in range(1, S):
        for r in (me, partner):
            pl.semaphore_signal(barrier, inc=1, device_id={"replica": r, "shard": lax.rem(shard + k, S)},
                                device_id_type=MESH)

    loads = []
    for k in range(chunks):
        trio = []
        for i, (src, dst) in enumerate(((lw, lw_v), (base, base_v), (ef, ef_v))):
            part = pl.ds(k * rows, rows)
            cp = pltpu.make_async_copy(src.at[part], dst.at[part], ld_sem.at[i, k])
            cp.start()
            trio.append(cp)
        loads.append(trio)
    own_in = pltpu.make_async_copy(mom, slots.at[me], mom_ld.at[0])
    own_in.start()
    tok_in = pltpu.make_async_copy(tok, tok_v, mom_ld.at[1])
    tok_in.start()

    def slot(b, hv):
        return slots.at[b, :, pl.ds(hv * span, span)]

    def own_copy(i, hv, target):
        return rcopy(slot(me, hv), slot(me, hv), own_send.at[i, hv], m_recv.at[me, hv], at_replica(target))

    def own_near(act, *parts):
        def go(i, target):
            for hv in parts:
                act(own_copy(i, hv, target))

        @pl.when(pos + 1 < L)
        def _():
            go(0, block_of(jnp.minimum(pos + 1, L - 1)))

        @pl.when(pos >= 1)
        def _():
            go(1, block_of(jnp.maximum(pos - 1, 0)))

    def own_to_partner(hv):
        return own_copy(2, hv, partner)

    def start(cp):
        cp.start()

    def finish_send(cp):
        cp.wait_send()

    def await_half(b, hv):
        rcopy(slot(b, hv), slot(b, hv), own_send.at[0, hv], m_recv.at[b, hv], at_replica(partner)).wait_recv()

    def passed_on(step, hv, act, wait, relays=(True, False)):
        for side, sign in enumerate((-1, 1)):
            origin = pos + sign * step
            nxt = pos - sign
            inner = (nxt >= 0) & (nxt < L)
            there = (origin >= 0) & (origin < L)
            if relays == (True,):
                there = there & inner
            if relays == (False,):
                there = there & jnp.logical_not(inner)

            @pl.when(there)
            def _():
                b = block_of(jnp.clip(origin, 0, L - 1))
                if wait:
                    await_half(b, hv)
                here = inner
                @pl.when(here)
                def _():
                    act(rcopy(slot(b, hv), slot(b, hv), fz_send.at[side, step - 1, hv], m_recv.at[b, hv],
                              at_replica(block_of(jnp.clip(nxt, 0, L - 1)))))

                act(rcopy(slot(b, hv), slot(b, hv), fp_send.at[side, step - 1, hv], m_recv.at[b, hv],
                          at_replica(partner)))

    def arrived(step, *parts, relays=(True, False)):
        if step < L:
            for hv in parts:
                passed_on(step, hv, start, True, relays)

    def token_rows(s):
        return pl.ds(pl.multiple_of(s * n, 128), n)

    def block_cols(bk):
        return pl.ds(pl.multiple_of(bk * 128, 128), 128)

    def a_copy(k, bk):
        target = lax.rem(shard + k, S)
        return rcopy(a_bf.at[token_rows(target), block_cols(bk)], a_in.at[shard, :, block_cols(bk)],
                     a_send.at[k, bk], a_recv.at[shard, bk], at_shard(target))

    def key_block(bk):
        cols = block_cols(bk)
        block = slots[pl.ds(bk * per, per)].reshape(128, d)
        a = a_buf[:, cols] - (outer_rate * outer_mu * outer_mu) * dot(tok_v[...], block, NT)
        a_buf[:, cols] = a
        a_bf[:, cols] = a.astype(BF16)
        for k in range(1, S):
            a_copy(k, bk).start()

    def turn_block(bk):
        cols = block_cols(bk)
        turned = slots[pl.ds(bk * per, per)].reshape(128, d).T
        v_buf[:, cols] = base_v[:, cols].astype(F32) - (outer_rate * outer_mu * outer_mu) * turned.astype(F32)

    def chip_block(p):
        for hv in range(HV):
            await_half(2 * p + 1 - core, hv)

    def blocks_at(step, *fs):
        if not 0 < step < L:
            return

        def side(i, carry):
            origin = pos + (2 * i - 1) * step

            @pl.when((origin >= 0) & (origin < L))
            def _():
                for f in fs:
                    f(jnp.clip(origin, 0, L - 1))

            return carry

        lax.fori_loop(0, 2, side, 0)

    keys_of = key_block if early else lambda p: None
    turn_of = turn_block if early else lambda p: None
    quarters = tuple(range(HV))

    qh, ql = split2(qt[...])
    q2 = jnp.concatenate([qh, ql], axis=0)
    for k in range(chunks):
        for cp in loads[k]:
            cp.wait()
        part = pl.ds(k * rows, rows)
        z = base_v[part, :].astype(F32) - lw_v[part, :].astype(F32) + ef_v[part, :].astype(F32)
        zf[part, :] = z
        high, low = split2(z)
        zh[part, :] = high
        both = dot(q2, high, NT)
        pt[:, part] = both[:rank] + (both[rank:] + dot(qh, low, NT))

    own_in.wait()
    pl.semaphore_wait(barrier, L + 2 * (S - 1))

    theirs = pl.ds(pl.multiple_of((1 - core) * h, 128), h)
    mine = pl.ds(pl.multiple_of(core * h, 128), h)
    pair = rcopy(pt.at[:, theirs], pair_in, pair_sem.at[0], pair_sem.at[1], at_replica(partner))
    pair.start()
    own_near(start, 0)
    pair.wait_recv()
    total = pt[:, mine] + pair_in[...]
    half[...] = total
    half_bf[...] = total.astype(BF16)

    def rs_copies(act):
        for j in range(nc):
            target = first_owner + j

            @pl.when(pos != target)
            def _():
                act(rcopy(half_bf.at[:, pl.ds(j * w, w)], rs_in.at[pos], rs_send.at[j], rs_recv.at[pos],
                          at_replica(block_of(target))))

    rs_copies(start)
    z_pair = rcopy(zh.at[theirs], zh_in, zx_sem.at[0], zx_sem.at[1], at_replica(partner))
    z_pair.start()
    for hv in quarters:
        own_to_partner(hv).start()
    own_near(start, *quarters[1:])

    owner = (pos >= first_owner) & (pos < first_owner + nc)
    own_index = jnp.clip(pos - first_owner, 0, nc - 1)

    def cols_of(cr, j):
        return pl.ds(pl.multiple_of(cr * h + j * w, 128), w)

    def fw_copy(cr, j):
        part = pm.at[:, cols_of(cr, j)]
        return rcopy(part, part, fw_send.at[j], ag_recv.at[cr, j], at_replica(partner))

    def ag_copy(k):
        part = pm.at[:, cols_of(core, own_index)]
        return rcopy(part, part, ag_send.at[k], ag_recv.at[core, own_index],
                     at_replica(block_of(lax.rem(pos + k, L))))

    tok_in.wait()
    a_buf[...] = dot(tok_v[...], base_v[...], NN)
    chip_block(pos)
    keys_of(pos)

    @pl.when(owner)
    def _():
        total = half[:, pl.ds(pl.multiple_of(own_index * w, 128), w)]
        for k in range(1, L):
            source = lax.rem(pos + k, L)
            rcopy(rs_in.at[source], rs_in.at[source], ag_send.at[k], rs_recv.at[source],
                  at_replica(partner)).wait_recv()
            total += rs_in[source].astype(F32)
        pm[:, cols_of(core, own_index)] = (total * (1.0 / R)).astype(BF16)
        for k in range(1, L):
            ag_copy(k).start()
        for j in range(nc):
            @pl.when(pos == first_owner + j)
            def _():
                fw_copy(core, j).start()

    z_pair.wait_recv()
    zs[...] = (zh[mine, :].astype(F32) + zh_in[...].astype(F32)).astype(BF16)
    arrived(1, *quarters[:-2])
    turn_of(pos)
    own_out[...] = slots[me]
    pick[...] = (lax.broadcasted_iota(jnp.int32, (kv, c), 0)
                 == me * c + lax.broadcasted_iota(jnp.int32, (kv, c), 1)).astype(BF16)
    arrived(1, quarters[-2])
    for j in range(nc):
        @pl.when(pos != first_owner + j)
        def _():
            fw_copy(core, j).wait_recv()
            fw_copy(core, j).start()

    tl[...] = dot(pm[:, mine], zs[...], NN)

    def tile_of(i):
        return (pl.ds(pl.multiple_of(lax.rem(i, groups) * 8, 8), 8),
                pl.ds(pl.multiple_of((i // groups) * wl, 128), wl))

    def if_owned(i, f):
        if tiles == plane:
            f()
        else:
            pl.when(i < tiles)(f)

    def t_copies(act):
        for k in range(1, plane):
            target = lax.rem(spot + k, plane)

            def go():
                a, b = tile_of(jnp.minimum(target, tiles - 1))
                act(rcopy(tl.at[a, b], t_in.at[spot], t_send.at[k], t_recv.at[spot], at_spot(target)))

            if_owned(target, go)

    t_copies(start)
    arrived(1, quarters[-1])
    arrived(2, quarters[0], relays=(True,))
    for j in range(nc):
        fw_copy(1 - core, j).wait_recv()
    gs[...] = jnp.zeros_like(gs)
    gs[:, 0:rank] = dot(pm[...], pm[...], NT)

    def g_copy(k):
        return rcopy(gs, g_in.at[shard], g_send.at[k], g_recv.at[shard], at_shard(lax.rem(shard + k, S)))

    for k in range(1, S):
        g_copy(k).start()
    my_spot = jnp.minimum(spot, tiles - 1)
    my_rows, my_cols = tile_of(my_spot)

    def z_copy(k):
        part = z_in.at[pos]
        return rcopy(part, part, z_send.at[k], z_recv.at[pos], at_replica(block_of(lax.rem(pos + k, L))))

    def sum_plane():
        total = tl[my_rows, my_cols]
        for k in range(1, plane):
            source = lax.rem(spot + k, plane)
            rcopy(t_in.at[source], t_in.at[source], t_send.at[k], t_recv.at[source], at_replica(partner)).wait_recv()
            total += t_in[source]
        z_in[pos] = total
        for k in range(1, L):
            z_copy(k).start()

    bt[...] = dot(pm[...], tok_v[...], NT)

    def b_copy(k):
        target = lax.rem(shard + k, S)
        return rcopy(bt.at[:, token_rows(target)], b_in.at[shard], b_send.at[k], b_recv.at[shard], at_shard(target))

    for k in range(1, S):
        b_copy(k).start()
    arrived(2, *quarters[1:-2], relays=(True,))
    if_owned(spot, sum_plane)
    arrived(2, *quarters[-2:], relays=(True,))
    arrived(2, quarters[0], relays=(False,))
    gram = gs[:, 0:rank]
    for k in range(1, S):
        source = lax.rem(shard + k, S)
        rcopy(g_in.at[source], g_in.at[source], g_send.at[k], g_recv.at[source], at_replica(partner)).wait_recv()
        gram = gram + g_in[source][:, 0:rank]
    inverse = invert(gram)
    blocks_at(1, chip_block, keys_of, turn_of)
    arrived(2, *quarters[1:-1], relays=(False,))

    def ta_copy(k):
        part = tt.at[my_rows, my_cols]
        return rcopy(part, part, ta_send.at[k], ta_recv.at[my_spot], at_spot(lax.rem(spot + k, plane)))

    def sum_planes():
        for k in range(1, L):
            source = lax.rem(pos + k, L)
            rcopy(z_in.at[source], z_in.at[source], z_send.at[k], z_recv.at[source], at_replica(partner)).wait_recv()
        total = z_in[0]
        for p in range(1, L):
            total += z_in[p]
        tt[my_rows, my_cols] = total * (1.0 / R)
        for k in range(1, plane):
            ta_copy(k).start()

    if_owned(spot, sum_planes)
    arrived(2, quarters[-1], relays=(False,))
    for step in range(2, L):
        if step > 2:
            arrived(step, *quarters)
        blocks_at(step, chip_block, keys_of)
    if not early:
        def late(bk, carry):
            key_block(bk)
            turn_block(bk)
            return carry

        lax.fori_loop(0, blocks, late, 0)

    pair.wait_send()
    z_pair.wait_send()
    rs_copies(finish_send)
    t_copies(finish_send)
    own_near(finish_send, *quarters)
    for hv in quarters:
        own_to_partner(hv).wait_send()
    for k in range(1, S):
        b_copy(k).wait_send()
        g_copy(k).wait_send()
    for j in range(nc):
        fw_copy(core, j).wait_send()

    def drain_z():
        for k in range(1, L):
            z_copy(k).wait_send()

    if_owned(spot, drain_z)

    @pl.when(owner)
    def _():
        for k in range(1, L):
            ag_copy(k).wait_send()

    for k in range(1, plane):
        source = lax.rem(spot + k, plane)

        def got():
            i = jnp.minimum(source, tiles - 1)
            a, b = tile_of(i)
            rcopy(tt.at[a, b], tt.at[a, b], ta_send.at[k], ta_recv.at[i], at_replica(partner)).wait_recv()

        if_owned(source, got)
    x = lax.dot_general(inverse, tt[...], NN, precision=HIGHEST, preferred_element_type=F32)
    high, low = split2(x)
    x2[...] = jnp.concatenate([high, low], axis=0)
    xo2[...] = dot(x2[...], pick[...], NN).astype(BF16)

    for step in range(2, L):
        blocks_at(step, turn_of)
    b_total = bt[:, token_rows(shard)]
    for k in range(1, S):
        source = lax.rem(shard + k, S)
        rcopy(b_in.at[source], b_in.at[source], b_send.at[k], b_recv.at[source], at_replica(partner)).wait_recv()
        b_total += b_in[source]
    total = a_buf[token_rows(shard), :] - (outer_rate * (outer_mu + 1.0)) * lax.dot_general(
        b_total, x, TN, precision=HIGHEST, preferred_element_type=F32)
    for hv in quarters:
        for step in range(1, L):
            passed_on(step, hv, finish_send, False)
    for k in range(1, S):
        source = lax.rem(shard + k, S)
        for bk in range(blocks):
            part = a_in.at[source, :, block_cols(bk)]
            rcopy(part, part, a_send.at[k, bk], a_recv.at[source, bk], at_replica(partner)).wait_recv()
        total += a_in[source].astype(F32)
    key_out[...] = total.astype(BF16)

    for k in range(1, S):
        for bk in range(blocks):
            a_copy(k, bk).wait_send()

    def drain_tile():
        for k in range(1, plane):
            ta_copy(k).wait_send()

    if_owned(spot, drain_tile)


def update_rows(pm, x2, xo2, zf, v, own, key, nb_out, nm_out, ne_out, key_out, nb, nm, ne, sem, rest):
    d = zf.shape[0]
    tile = min(256, d)
    copies = [pltpu.make_async_copy(key, key_out, rest.at[0])]
    copies[0].start()
    for t in range(d // tile):
        part = pl.ds(t * tile, tile)
        p = pm[:, part]
        p2 = jnp.concatenate([p, p], axis=0)
        u = dot(p2, x2[...], TN)
        ne[part, :] = (zf[part, :] - u).astype(BF16)
        nb[part, :] = (v[part, :] - (outer_rate * (outer_mu + 1.0)) * u).astype(BF16)
        for i, (held, out) in enumerate(((ne, ne_out), (nb, nb_out))):
            cp = pltpu.make_async_copy(held.at[part], out.at[part], sem.at[i, t])
            cp.start()
            copies.append(cp)
        if t == 0:
            whole = pm[...]
            nm[...] = (outer_mu * own[...].astype(F32)
                       + dot(xo2[...], jnp.concatenate([whole, whole], axis=0), TN)).astype(BF16)
            cp = pltpu.make_async_copy(nm, nm_out, rest.at[1])
            cp.start()
            copies.append(cp)
    for cp in copies:
        cp.wait()


def on_device(local_weights, outer_base, momentum, error_feedback, q_start, tokens):
    R = lax.axis_size("replica")
    S = lax.axis_size("shard")
    d, kv = outer_base.shape
    rank = q_start.shape[1]
    c = momentum.shape[1]
    L = R // 2
    lw, ef, tok = local_weights[0], error_feedback[0], tokens[0]
    nt = tok.shape[0]
    n = nt // S
    blocks = kv // 128
    chunks = min(4, d // 128)
    h, nc, w, groups, tiles, wl = sizes(d, kv, rank, S)
    HV = HALVES
    V = pltpu.VMEM
    dma = pltpu.SemaphoreType.DMA
    hbm = pl.BlockSpec(memory_space=pltpu.HBM)
    anywhere = pl.BlockSpec(memory_space=pl.ANY)
    vm = pl.BlockSpec(memory_space=pltpu.VMEM)
    shapes = ((d, kv), (c, d), (d, kv), (n, kv))
    tiles_out = d // min(256, d)
    passed = ((rank, d), BF16), ((2 * rank, kv), BF16), ((2 * rank, c), BF16), ((d, kv), F32), ((d, kv), F32), ((c, d), BF16), ((n, kv), BF16)
    held = pl.pallas_call(
        functools.partial(exchange, (R, S, d, kv, rank)),
        out_shape=tuple(pltpu.VMEM(s, t) for s, t in passed),
        in_specs=[hbm, hbm, hbm, vm, hbm, hbm],
        out_specs=(vm,) * len(passed),
        scratch_shapes=[
            V((d, kv), BF16), V((d, kv), BF16), V((d, kv), BF16), V((d, kv), BF16), V((h, kv), BF16), V((h, kv), BF16),
            V((nt, d), BF16), V((R, c, d), BF16), V((kv, c), BF16),
            V((rank, d), F32), V((rank, h), F32), V((rank, h), F32), V((rank, h), BF16), V((L, rank, w), BF16),
            V((rank, 128), F32), V((S, rank, 128), F32),
            V((rank, kv), F32), V((2 * S, 8, wl), F32), V((L, 8, wl), F32), V((rank, kv), F32),
            V((nt, kv), F32), V((nt, kv), BF16), V((S, n, kv), BF16), V((rank, nt), F32), V((S, rank, n), F32),
            dma((3, chunks)), dma((2,)), dma((2,)), dma((2,)), dma((nc,)), dma((L,)), dma((L,)), dma((2, nc)), dma((nc,)),
            dma((S,)), dma((S,)), dma((2 * S,)), dma((2 * S,)), dma((L,)), dma((L,)), dma((2 * S,)), dma((tiles,)),
            dma((4, HV)), dma((2, L, HV)), dma((2, L, HV)), dma((R, HV)),
            dma((S, blocks)), dma((S, blocks)), dma((S,)), dma((S,)),
        ],
        compiler_params=pltpu.CompilerParams(collective_id=0, has_side_effects=True, vmem_limit_bytes=48 << 20),
        name="exchange",
    )(lw, outer_base, ef, q_start.T, momentum.T, tok)
    nb, nm, ne, keys = pl.pallas_call(
        update_rows,
        out_shape=tuple(jax.ShapeDtypeStruct(s, BF16) for s in shapes),
        in_specs=[vm] * len(passed),
        out_specs=(anywhere,) * 4,
        scratch_shapes=[V(s, BF16) for s in shapes[:3]] + [dma((2, tiles_out)), dma((2,))],
        compiler_params=pltpu.CompilerParams(vmem_limit_bytes=16 << 20),
        name="update_rows",
    )(*held)
    return nb, nm.T, ne[None], keys[None]


def solution(mesh):
    in_specs = (
        P("replica", "shard", None),
        P("shard", None),
        P("shard", "replica"),
        P("replica", "shard", None),
        P(),
        P("replica", None, "shard"),
    )
    out_specs = (
        P("shard", None),
        P("shard", "replica"),
        P("replica", "shard", None),
        P("replica", "shard", None),
    )
    return jax.shard_map(
        on_device, mesh=mesh, in_specs=in_specs, out_specs=out_specs, check_vma=False
    )
```

```python
import functools

import jax
import jax.numpy as jnp
from jax import lax
from jax.experimental import pallas as pl
from jax.experimental.pallas import tpu as pltpu
from jax.sharding import PartitionSpec as P

outer_mu = 0.9
outer_rate = 0.7
MESH = pl.DeviceIdType.MESH
F32 = jnp.float32
BF16 = jnp.bfloat16
NT = (((1,), (1,)), ((), ()))
NN = (((1,), (0,)), ((), ()))
TN = (((0,), (0,)), ((), ()))
HIGHEST = lax.Precision.HIGHEST
HALVES = 4


def dot(a, b, dims):
    return lax.dot_general(a, b, dims, preferred_element_type=F32)


def split2(x):
    high = x.astype(BF16)
    return high, (x - high.astype(F32)).astype(BF16)


def invert(a):
    n = a.shape[0]
    rows = lax.broadcasted_iota(jnp.int32, (n, n), 0)
    cols = lax.broadcasted_iota(jnp.int32, (n, n), 1)
    lane = lax.broadcasted_iota(jnp.int32, (1, n), 1)
    for k in range(n):
        inverse_pivot = 1.0 / a[k : k + 1, k : k + 1]
        col = a[:, k : k + 1]
        row = jnp.where(lane == k, 1.0, a[k : k + 1, :]) * inverse_pivot
        a = jnp.where(rows == k, row, jnp.where(cols == k, 0.0, a) - col * row)
    return a


def sizes(d, kv, rank, S):
    h = d // 2
    nc = 2 if h % 256 == 0 else 1
    groups = rank // 8
    tiles = min(2 * S, groups * (kv // 128))
    return h, nc, h // nc, groups, tiles, kv // (tiles // groups)


def exchange(cfg, lw, base, ef, qt, mom, tok, pm, x2, xo2, zf, v_buf, own_out, key_out,
             lw_v, base_v, ef_v, zh, zh_in, zs, tok_v, slots, pick,
             pt, pair_in, half, half_bf, rs_in, gs, g_in,
             tl, t_in, z_in, tt, a_buf, a_bf, a_in, bt, b_in,
             ld_sem, mom_ld, pair_sem, zx_sem, rs_send, rs_recv, ag_send, ag_recv, fw_send,
             g_send, g_recv, t_send, t_recv, z_send, z_recv, ta_send, ta_recv,
             own_send, fz_send, fp_send, m_recv, a_send, a_recv, b_send, b_recv):
    R, S, d, kv, rank = cfg
    L = R // 2
    me = lax.axis_index("replica")
    shard = lax.axis_index("shard")
    core = lax.rem(me, 2)
    pos = me // 2
    partner = me + 1 - 2 * core
    chunks = ld_sem.shape[1]
    rows = d // chunks
    h, nc, w, groups, tiles, wl = sizes(d, kv, rank, S)
    first_owner = L // 2 - nc // 2
    c = slots.shape[1]
    per = 128 // c
    blocks = kv // 128
    n = tok_v.shape[0] // S
    early = per == 2
    HV = HALVES
    span = d // HV
    plane = 2 * S
    spot = 2 * shard + core

    def at_replica(r):
        return {"replica": r}

    def at_shard(s):
        return {"shard": s}

    def at_spot(i):
        return {"replica": 2 * pos + lax.rem(i, 2), "shard": i // 2}

    def block_of(p):
        return 2 * p + core

    def rcopy(src, dst, ss, rs, dev):
        return pltpu.make_async_remote_copy(src_ref=src, dst_ref=dst, send_sem=ss, recv_sem=rs,
                                            device_id=dev, device_id_type=MESH)

    barrier = pltpu.get_barrier_semaphore()
    for k in range(1, R):
        pl.semaphore_signal(barrier, inc=1, device_id=at_replica(lax.rem(me + k, R)), device_id_type=MESH)
    for k in range(1, S):
        for r in (me, partner):
            pl.semaphore_signal(barrier, inc=1, device_id={"replica": r, "shard": lax.rem(shard + k, S)},
                                device_id_type=MESH)

    loads = []
    for k in range(chunks):
        trio = []
        for i, (src, dst) in enumerate(((lw, lw_v), (base, base_v), (ef, ef_v))):
            part = pl.ds(k * rows, rows)
            cp = pltpu.make_async_copy(src.at[part], dst.at[part], ld_sem.at[i, k])
            cp.start()
            trio.append(cp)
        loads.append(trio)
    own_in = pltpu.make_async_copy(mom, slots.at[me], mom_ld.at[0])
    own_in.start()
    tok_in = pltpu.make_async_copy(tok, tok_v, mom_ld.at[1])
    tok_in.start()

    def slot(b, hv):
        return slots.at[b, :, pl.ds(hv * span, span)]

    def own_copy(i, hv, target):
        return rcopy(slot(me, hv), slot(me, hv), own_send.at[i, hv], m_recv.at[me, hv], at_replica(target))

    def own_near(act, *parts):
        def go(i, target):
            for hv in parts:
                act(own_copy(i, hv, target))

        @pl.when(pos + 1 < L)
        def _():
            go(0, block_of(jnp.minimum(pos + 1, L - 1)))

        @pl.when(pos >= 1)
        def _():
            go(1, block_of(jnp.maximum(pos - 1, 0)))

    def own_to_partner(hv):
        return own_copy(2, hv, partner)

    def start(cp):
        cp.start()

    def finish_send(cp):
        cp.wait_send()

    def await_half(b, hv):
        rcopy(slot(b, hv), slot(b, hv), own_send.at[0, hv], m_recv.at[b, hv], at_replica(partner)).wait_recv()

    def passed_on(step, hv, act, wait, relays=(True, False)):
        for side, sign in enumerate((-1, 1)):
            origin = pos + sign * step
            nxt = pos - sign
            inner = (nxt >= 0) & (nxt < L)
            there = (origin >= 0) & (origin < L)
            if relays == (True,):
                there = there & inner
            if relays == (False,):
                there = there & jnp.logical_not(inner)

            @pl.when(there)
            def _():
                b = block_of(jnp.clip(origin, 0, L - 1))
                if wait:
                    await_half(b, hv)
                here = inner
                @pl.when(here)
                def _():
                    act(rcopy(slot(b, hv), slot(b, hv), fz_send.at[side, step - 1, hv], m_recv.at[b, hv],
                              at_replica(block_of(jnp.clip(nxt, 0, L - 1)))))

                act(rcopy(slot(b, hv), slot(b, hv), fp_send.at[side, step - 1, hv], m_recv.at[b, hv],
                          at_replica(partner)))

    def arrived(step, *parts, relays=(True, False)):
        if step < L:
            for hv in parts:
                passed_on(step, hv, start, True, relays)

    def token_rows(s):
        return pl.ds(pl.multiple_of(s * n, 128), n)

    def block_cols(bk):
        return pl.ds(pl.multiple_of(bk * 128, 128), 128)

    def a_copy(k, bk):
        target = lax.rem(shard + k, S)
        return rcopy(a_bf.at[token_rows(target), block_cols(bk)], a_in.at[shard, :, block_cols(bk)],
                     a_send.at[k, bk], a_recv.at[shard, bk], at_shard(target))

    def key_block(bk):
        cols = block_cols(bk)
        block = slots[pl.ds(bk * per, per)].reshape(128, d)
        a = a_buf[:, cols] - (outer_rate * outer_mu * outer_mu) * dot(tok_v[...], block, NT)
        a_buf[:, cols] = a
        a_bf[:, cols] = a.astype(BF16)
        for k in range(1, S):
            a_copy(k, bk).start()

    def turn_block(bk):
        cols = block_cols(bk)
        turned = slots[pl.ds(bk * per, per)].reshape(128, d).T
        v_buf[:, cols] = base_v[:, cols].astype(F32) - (outer_rate * outer_mu * outer_mu) * turned.astype(F32)

    def chip_block(p):
        for hv in range(HV):
            await_half(2 * p + 1 - core, hv)

    def blocks_at(step, *fs):
        if not 0 < step < L:
            return

        def side(i, carry):
            origin = pos + (2 * i - 1) * step

            @pl.when((origin >= 0) & (origin < L))
            def _():
                for f in fs:
                    f(jnp.clip(origin, 0, L - 1))

            return carry

        lax.fori_loop(0, 2, side, 0)

    keys_of = key_block if early else lambda p: None
    turn_of = turn_block if early else lambda p: None
    quarters = tuple(range(HV))

    outer = jnp.where(pos < L // 2, jnp.where(pos > 0, pos - 1, min(1, L - 1)),
                      jnp.where(pos < L - 1, pos + 1, max(L - 2, 0)))
    inner_block = 2 * pos - outer

    def take_outer(*fs):
        if L > 1:
            for f in fs:
                f(outer)

    def take_inner(*fs):
        if L > 1:
            @pl.when((inner_block >= 0) & (inner_block < L))
            def _():
                for f in fs:
                    f(jnp.clip(inner_block, 0, L - 1))

    qh, ql = split2(qt[...])
    q2 = jnp.concatenate([qh, ql], axis=0)
    for k in range(chunks):
        for cp in loads[k]:
            cp.wait()
        part = pl.ds(k * rows, rows)
        z = base_v[part, :].astype(F32) - lw_v[part, :].astype(F32) + ef_v[part, :].astype(F32)
        zf[part, :] = z
        high, low = split2(z)
        zh[part, :] = high
        both = dot(q2, high, NT)
        pt[:, part] = both[:rank] + (both[rank:] + dot(qh, low, NT))

    own_in.wait()
    pl.semaphore_wait(barrier, R - 1 + 2 * (S - 1))

    theirs = pl.ds(pl.multiple_of((1 - core) * h, 128), h)
    mine = pl.ds(pl.multiple_of(core * h, 128), h)
    pair = rcopy(pt.at[:, theirs], pair_in, pair_sem.at[0], pair_sem.at[1], at_replica(partner))
    pair.start()
    own_near(start, 0)
    z_pair = rcopy(zh.at[theirs], zh_in, zx_sem.at[0], zx_sem.at[1], at_replica(partner))
    z_pair.start()
    for hv in quarters:
        own_to_partner(hv).start()
    pair.wait_recv()
    total = pt[:, mine] + pair_in[...]
    half[...] = total
    half_bf[...] = total.astype(BF16)

    def rs_copies(act):
        for j in range(nc):
            target = first_owner + j

            @pl.when(pos != target)
            def _():
                act(rcopy(half_bf.at[:, pl.ds(j * w, w)], rs_in.at[pos], rs_send.at[j], rs_recv.at[pos],
                          at_replica(block_of(target))))

    rs_copies(start)
    own_near(start, *quarters[1:])

    owner = (pos >= first_owner) & (pos < first_owner + nc)
    own_index = jnp.clip(pos - first_owner, 0, nc - 1)

    def cols_of(cr, j):
        return pl.ds(pl.multiple_of(cr * h + j * w, 128), w)

    def fw_copy(cr, j):
        part = pm.at[:, cols_of(cr, j)]
        return rcopy(part, part, fw_send.at[j], ag_recv.at[cr, j], at_replica(partner))

    def ag_copy(k):
        part = pm.at[:, cols_of(core, own_index)]
        return rcopy(part, part, ag_send.at[k], ag_recv.at[core, own_index],
                     at_replica(block_of(lax.rem(pos + k, L))))

    tok_in.wait()
    a_buf[...] = dot(tok_v[...], base_v[...], NN)
    chip_block(pos)
    keys_of(pos)

    @pl.when(owner)
    def _():
        total = half[:, pl.ds(pl.multiple_of(own_index * w, 128), w)]
        for k in range(1, L):
            source = lax.rem(pos + k, L)
            rcopy(rs_in.at[source], rs_in.at[source], ag_send.at[k], rs_recv.at[source],
                  at_replica(partner)).wait_recv()
            total += rs_in[source].astype(F32)
        pm[:, cols_of(core, own_index)] = (total * (1.0 / R)).astype(BF16)
        for k in range(1, L):
            ag_copy(k).start()
        for j in range(nc):
            @pl.when(pos == first_owner + j)
            def _():
                fw_copy(core, j).start()

    z_pair.wait_recv()
    zs[...] = (zh[mine, :].astype(F32) + zh_in[...].astype(F32)).astype(BF16)
    arrived(1, *quarters[:-2])
    turn_of(pos)
    own_out[...] = slots[me]
    pick[...] = (lax.broadcasted_iota(jnp.int32, (kv, c), 0)
                 == me * c + lax.broadcasted_iota(jnp.int32, (kv, c), 1)).astype(BF16)
    arrived(1, quarters[-2])
    for j in range(nc):
        @pl.when(pos != first_owner + j)
        def _():
            fw_copy(core, j).wait_recv()
            fw_copy(core, j).start()

    tl[...] = dot(pm[:, mine], zs[...], NN)

    def tile_of(i):
        return (pl.ds(pl.multiple_of(lax.rem(i, groups) * 8, 8), 8),
                pl.ds(pl.multiple_of((i // groups) * wl, 128), wl))

    def if_owned(i, f):
        if tiles == plane:
            f()
        else:
            pl.when(i < tiles)(f)

    def t_copies(act):
        for k in range(1, plane):
            target = lax.rem(spot + k, plane)

            def go():
                a, b = tile_of(jnp.minimum(target, tiles - 1))
                act(rcopy(tl.at[a, b], t_in.at[spot], t_send.at[k], t_recv.at[spot], at_spot(target)))

            if_owned(target, go)

    t_copies(start)
    arrived(1, quarters[-1])
    arrived(2, quarters[0], relays=(True,))
    for j in range(nc):
        fw_copy(1 - core, j).wait_recv()
    gs[...] = jnp.zeros_like(gs)
    gs[:, 0:rank] = dot(pm[...], pm[...], NT)

    def g_copy(k):
        return rcopy(gs, g_in.at[shard], g_send.at[k], g_recv.at[shard], at_shard(lax.rem(shard + k, S)))

    for k in range(1, S):
        g_copy(k).start()
    my_spot = jnp.minimum(spot, tiles - 1)
    my_rows, my_cols = tile_of(my_spot)

    def z_copy(k):
        part = z_in.at[pos]
        return rcopy(part, part, z_send.at[k], z_recv.at[pos], at_replica(block_of(lax.rem(pos + k, L))))

    def sum_plane():
        total = tl[my_rows, my_cols]
        for k in range(1, plane):
            source = lax.rem(spot + k, plane)
            rcopy(t_in.at[source], t_in.at[source], t_send.at[k], t_recv.at[source], at_replica(partner)).wait_recv()
            total += t_in[source]
        z_in[pos] = total
        for k in range(1, L):
            z_copy(k).start()

    bt[...] = dot(pm[...], tok_v[...], NT)

    def b_copy(k):
        target = lax.rem(shard + k, S)
        return rcopy(bt.at[:, token_rows(target)], b_in.at[shard], b_send.at[k], b_recv.at[shard], at_shard(target))

    for k in range(1, S):
        b_copy(k).start()
    arrived(2, *quarters[1:-2], relays=(True,))
    if_owned(spot, sum_plane)
    take_outer(chip_block, keys_of)
    arrived(2, *quarters[-2:], relays=(True,))
    arrived(2, quarters[0], relays=(False,))
    gram = gs[:, 0:rank]
    for k in range(1, S):
        source = lax.rem(shard + k, S)
        rcopy(g_in.at[source], g_in.at[source], g_send.at[k], g_recv.at[source], at_replica(partner)).wait_recv()
        gram = gram + g_in[source][:, 0:rank]
    inverse = invert(gram)
    take_outer(turn_of)
    arrived(2, *quarters[1:-1], relays=(False,))

    def ta_copy(k):
        part = tt.at[my_rows, my_cols]
        return rcopy(part, part, ta_send.at[k], ta_recv.at[my_spot], at_spot(lax.rem(spot + k, plane)))

    def sum_planes():
        for k in range(1, L):
            source = lax.rem(pos + k, L)
            rcopy(z_in.at[source], z_in.at[source], z_send.at[k], z_recv.at[source], at_replica(partner)).wait_recv()
        total = z_in[0]
        for p in range(1, L):
            total += z_in[p]
        tt[my_rows, my_cols] = total * (1.0 / R)
        for k in range(1, plane):
            ta_copy(k).start()

    if_owned(spot, sum_planes)
    arrived(2, quarters[-1], relays=(False,))
    take_inner(chip_block, keys_of, turn_of)
    for step in range(2, L):
        if step > 2:
            arrived(step, *quarters)
        blocks_at(step, chip_block, keys_of, turn_of)
    if not early:
        def late(bk, carry):
            key_block(bk)
            turn_block(bk)
            return carry

        lax.fori_loop(0, blocks, late, 0)

    pair.wait_send()
    z_pair.wait_send()
    rs_copies(finish_send)
    t_copies(finish_send)
    own_near(finish_send, *quarters)
    for hv in quarters:
        own_to_partner(hv).wait_send()
    for k in range(1, S):
        b_copy(k).wait_send()
        g_copy(k).wait_send()
    for j in range(nc):
        fw_copy(core, j).wait_send()

    def drain_z():
        for k in range(1, L):
            z_copy(k).wait_send()

    if_owned(spot, drain_z)

    @pl.when(owner)
    def _():
        for k in range(1, L):
            ag_copy(k).wait_send()

    for k in range(1, plane):
        source = lax.rem(spot + k, plane)

        def got():
            i = jnp.minimum(source, tiles - 1)
            a, b = tile_of(i)
            rcopy(tt.at[a, b], tt.at[a, b], ta_send.at[k], ta_recv.at[i], at_replica(partner)).wait_recv()

        if_owned(source, got)
    x = lax.dot_general(inverse, tt[...], NN, precision=HIGHEST, preferred_element_type=F32)
    high, low = split2(x)
    x2[...] = jnp.concatenate([high, low], axis=0)
    xo2[...] = dot(x2[...], pick[...], NN).astype(BF16)

    b_total = bt[:, token_rows(shard)]
    for k in range(1, S):
        source = lax.rem(shard + k, S)
        rcopy(b_in.at[source], b_in.at[source], b_send.at[k], b_recv.at[source], at_replica(partner)).wait_recv()
        b_total += b_in[source]
    total = a_buf[token_rows(shard), :] - (outer_rate * (outer_mu + 1.0)) * lax.dot_general(
        b_total, x, TN, precision=HIGHEST, preferred_element_type=F32)
    for hv in quarters:
        for step in range(1, L):
            passed_on(step, hv, finish_send, False)
    for k in range(1, S):
        source = lax.rem(shard + k, S)
        for bk in range(blocks):
            part = a_in.at[source, :, block_cols(bk)]
            rcopy(part, part, a_send.at[k, bk], a_recv.at[source, bk], at_replica(partner)).wait_recv()
        total += a_in[source].astype(F32)
    key_out[...] = total.astype(BF16)

    for k in range(1, S):
        for bk in range(blocks):
            a_copy(k, bk).wait_send()

    def drain_tile():
        for k in range(1, plane):
            ta_copy(k).wait_send()

    if_owned(spot, drain_tile)


def update_rows(pm, x2, xo2, zf, v, own, key, nb_out, nm_out, ne_out, key_out, nb, nm, ne, sem, rest):
    d = zf.shape[0]
    tile = min(256, d)
    copies = [pltpu.make_async_copy(key, key_out, rest.at[0])]
    copies[0].start()
    for t in range(d // tile):
        part = pl.ds(t * tile, tile)
        p = pm[:, part]
        p2 = jnp.concatenate([p, p], axis=0)
        u = dot(p2, x2[...], TN)
        ne[part, :] = (zf[part, :] - u).astype(BF16)
        nb[part, :] = (v[part, :] - (outer_rate * (outer_mu + 1.0)) * u).astype(BF16)
        for i, (held, out) in enumerate(((ne, ne_out), (nb, nb_out))):
            cp = pltpu.make_async_copy(held.at[part], out.at[part], sem.at[i, t])
            cp.start()
            copies.append(cp)
        if t == 0:
            whole = pm[...]
            nm[...] = (outer_mu * own[...].astype(F32)
                       + dot(xo2[...], jnp.concatenate([whole, whole], axis=0), TN)).astype(BF16)
            cp = pltpu.make_async_copy(nm, nm_out, rest.at[1])
            cp.start()
            copies.append(cp)
    for cp in copies:
        cp.wait()


def on_device(local_weights, outer_base, momentum, error_feedback, q_start, tokens):
    R = lax.axis_size("replica")
    S = lax.axis_size("shard")
    d, kv = outer_base.shape
    rank = q_start.shape[1]
    c = momentum.shape[1]
    L = R // 2
    lw, ef, tok = local_weights[0], error_feedback[0], tokens[0]
    nt = tok.shape[0]
    n = nt // S
    blocks = kv // 128
    chunks = min(4, d // 128)
    h, nc, w, groups, tiles, wl = sizes(d, kv, rank, S)
    HV = HALVES
    V = pltpu.VMEM
    dma = pltpu.SemaphoreType.DMA
    hbm = pl.BlockSpec(memory_space=pltpu.HBM)
    anywhere = pl.BlockSpec(memory_space=pl.ANY)
    vm = pl.BlockSpec(memory_space=pltpu.VMEM)
    shapes = ((d, kv), (c, d), (d, kv), (n, kv))
    tiles_out = d // min(256, d)
    passed = ((rank, d), BF16), ((2 * rank, kv), BF16), ((2 * rank, c), BF16), ((d, kv), F32), ((d, kv), F32), ((c, d), BF16), ((n, kv), BF16)
    held = pl.pallas_call(
        functools.partial(exchange, (R, S, d, kv, rank)),
        out_shape=tuple(pltpu.VMEM(s, t) for s, t in passed),
        in_specs=[hbm, hbm, hbm, vm, hbm, hbm],
        out_specs=(vm,) * len(passed),
        scratch_shapes=[
            V((d, kv), BF16), V((d, kv), BF16), V((d, kv), BF16), V((d, kv), BF16), V((h, kv), BF16), V((h, kv), BF16),
            V((nt, d), BF16), V((R, c, d), BF16), V((kv, c), BF16),
            V((rank, d), F32), V((rank, h), F32), V((rank, h), F32), V((rank, h), BF16), V((L, rank, w), BF16),
            V((rank, 128), F32), V((S, rank, 128), F32),
            V((rank, kv), F32), V((2 * S, 8, wl), F32), V((L, 8, wl), F32), V((rank, kv), F32),
            V((nt, kv), F32), V((nt, kv), BF16), V((S, n, kv), BF16), V((rank, nt), F32), V((S, rank, n), F32),
            dma((3, chunks)), dma((2,)), dma((2,)), dma((2,)), dma((nc,)), dma((L,)), dma((L,)), dma((2, nc)), dma((nc,)),
            dma((S,)), dma((S,)), dma((2 * S,)), dma((2 * S,)), dma((L,)), dma((L,)), dma((2 * S,)), dma((tiles,)),
            dma((4, HV)), dma((2, L, HV)), dma((2, L, HV)), dma((R, HV)),
            dma((S, blocks)), dma((S, blocks)), dma((S,)), dma((S,)),
        ],
        compiler_params=pltpu.CompilerParams(collective_id=0, has_side_effects=True, vmem_limit_bytes=48 << 20),
        name="exchange",
    )(lw, outer_base, ef, q_start.T, momentum.T, tok)
    nb, nm, ne, keys = pl.pallas_call(
        update_rows,
        out_shape=tuple(jax.ShapeDtypeStruct(s, BF16) for s in shapes),
        in_specs=[vm] * len(passed),
        out_specs=(anywhere,) * 4,
        scratch_shapes=[V(s, BF16) for s in shapes[:3]] + [dma((2, tiles_out)), dma((2,))],
        compiler_params=pltpu.CompilerParams(vmem_limit_bytes=16 << 20),
        name="update_rows",
    )(*held)
    return nb, nm.T, ne[None], keys[None]


def solution(mesh):
    in_specs = (
        P("replica", "shard", None),
        P("shard", None),
        P("shard", "replica"),
        P("replica", "shard", None),
        P(),
        P("replica", None, "shard"),
    )
    out_specs = (
        P("shard", None),
        P("shard", "replica"),
        P("replica", "shard", None),
        P("replica", "shard", None),
    )
    return jax.shard_map(
        on_device, mesh=mesh, in_specs=in_specs, out_specs=out_specs, check_vma=False
    )
```
